512 devices in a mesh: crate: 32 (over z, x), board: 16 (over y, core).
Axes of the slice: x: 4, y: 8, z: 8, core: 2. Of those that a mesh axis runs over, the one named last changes fastest.
Arguments:
- voltages: bfloat16 [2048, 65536], P(('crate', 'board')), may hold values from -6 to 6
- wiring: int32 [2048], replicated, may hold values from 0 to 2047, each once
- positions: float32 [2, 2048], replicated, may hold values from -4 to 4
- directions: float32 [2, 512], replicated, may hold values from -1 to 1
- gains: float32 [2, 256, 2048], P(None, 'crate'), may hold values from -6 to 6
- delays: int32 [256, 512], replicated, may hold values from 0 to 31
Outputs:
- dedispersed: float32 [512, 512, 32], P('crate', 'board')
The draws below stay inside these ranges and needn't reach their ends.
Inputs may be any that keep to these rules, and one draw needn't show every extreme that they name: `wiring`: each of the 2048 antennas is wired to exactly one input row.
All inputs are finite; a program needn't handle non-finite values.
Results may differ from the reference program's by a relative error of at most 0.0096.
Values may be sent and summed in bfloat16 or wider, within the bound.
A program may use at most 64 MiB of HBM per device.

```python
import math
import jax
import jax.numpy as jnp
from jax import lax

ANTENNA_INPUTS = 2048
FREQ_CHANNELS = 256
FRAME_SAMPLES = 512
BEAMS = 512
DMS = 512
SPECTRUM_BATCHES = 2
BATCH_SPECTRA = 64
AVG = 4
TB = 32


def with_ends(drawn, own_key, smallest, high):
    shape = drawn.shape
    index_at = [jax.random.randint(jax.random.fold_in(own_key, axis), (), 0, shape[axis]) for axis in range(len(shape))]
    drawn = drawn.at[tuple(index_at)].set(smallest)
    longest = shape.index(max(shape))
    index_at[longest] = (index_at[longest] + 1) % shape[longest]
    return drawn.at[tuple(index_at)].set(high)


def block_levels(own_key, shape, pieces, smallest, high):
    gain, own = 1.0, jax.random.fold_in(own_key, 6)
    for position, shards_of in pieces:
        steps = jnp.exp(jax.random.uniform(jax.random.fold_in(own, position), (shards_of,), jnp.float32, smallest / len(pieces), high / len(pieces)))
        gain = gain * jnp.repeat(steps, shape[position] // shards_of).reshape([-1 if axis == position else 1 for axis in range(len(shape))])
    return gain


def normal_values(own_key, dims, width, most, shards=(), held_as=jnp.bfloat16):
    result = jax.random.normal(own_key, dims, jnp.float32) * width
    if len(shards) > 0:
        result = block_levels(own_key, dims, shards, -0.22, 0.18) * result
    return jnp.clip(result, min=-most, max=most).astype(held_as)


def setup_inputs(seed: int = 0) -> dict:
    arg_keys = jax.random.split(jax.random.key(seed), 7)
    voltages = normal_values(arg_keys[0], (ANTENNA_INPUTS, SPECTRUM_BATCHES * BATCH_SPECTRA * FRAME_SAMPLES), 1.0, 6.0, ((0, 512),))
    wiring = jax.random.permutation(arg_keys[1], ANTENNA_INPUTS).astype(jnp.int32)
    positions = jnp.clip(jax.random.uniform(arg_keys[2], (2, ANTENNA_INPUTS), jnp.float32, -4.0, 4.0), -4.0, 4.0)
    directions = jnp.clip(jax.random.uniform(arg_keys[3], (2, BEAMS), jnp.float32, -1.0, 1.0), -1.0, 1.0)
    gains = normal_values(arg_keys[4], (2, FREQ_CHANNELS, ANTENNA_INPUTS), 1.0, 6.0, ((1, 32),), jnp.float32)
    delays = with_ends(jax.random.randint(arg_keys[5], (FREQ_CHANNELS, DMS), 0, TB), jax.random.fold_in(arg_keys[5], 1), 0, TB - 1).astype(jnp.int32)
    return dict(voltages=voltages, wiring=wiring, positions=positions, directions=directions, gains=gains, delays=delays)


two_pi = 2.0 * math.pi

def filter_table():
    sample_ids = jnp.arange(FRAME_SAMPLES, dtype=jnp.int32)
    column_ids = jnp.arange(FREQ_CHANNELS, dtype=jnp.int32)
    window = 0.5 - 0.5 * jnp.cos(two_pi / FRAME_SAMPLES * sample_ids.astype(jnp.float32))
    turn_ids = sample_ids[:, None] * column_ids[None, :] % FRAME_SAMPLES
    phase_angle = two_pi / FRAME_SAMPLES * turn_ids.astype(jnp.float32)
    scale_norm_factor = 1.0 / math.sqrt(3.0 * FRAME_SAMPLES / 8.0)
    real_part = window[:, None] * jnp.cos(phase_angle) * scale_norm_factor
    imag_part = -window[:, None] * jnp.sin(phase_angle) * scale_norm_factor
    return jnp.concatenate([real_part, imag_part], axis=1).astype(jnp.bfloat16)

def beam_weights(channel, directions, place_x, place_y, gain_re, gain_im):
    geo_delay = directions[0][:, None] * place_x[None, :] + directions[1][:, None] * place_y[None, :]
    factor = two_pi * (1.0 + channel.astype(jnp.float32) / FREQ_CHANNELS)
    phase_angle = factor * geo_delay
    cosine = jnp.cos(phase_angle)
    sine_value = jnp.sin(phase_angle)
    scale_norm_factor = 1.0 / math.sqrt(ANTENNA_INPUTS)
    weight_re = ((gain_re[None, :] * cosine + gain_im[None, :] * sine_value) * scale_norm_factor).astype(jnp.bfloat16)
    weight_im = ((gain_im[None, :] * cosine - gain_re[None, :] * sine_value) * scale_norm_factor).astype(jnp.bfloat16)
    return (weight_re, weight_im)

def inverse_series(freq_re, freq_im):
    count_bins = freq_re.shape[0]
    index_ids = jnp.arange(count_bins, dtype=jnp.int32)
    turn_ids = index_ids[:, None] * index_ids[None, :] % count_bins
    phase_angle = two_pi / count_bins * turn_ids.astype(jnp.float32)
    keep_mask = (index_ids > 0).astype(jnp.float32)[:, None]
    scale_norm_factor = 1.0 / (count_bins * math.sqrt(FREQ_CHANNELS))
    cos_table = jnp.cos(phase_angle) * keep_mask
    sin_table = jnp.sin(phase_angle) * keep_mask
    first_term = jnp.einsum('kdb,kt->bdt', freq_re, cos_table, precision=lax.Precision.HIGHEST)
    second_term = jnp.einsum('kdb,kt->bdt', freq_im, sin_table, precision=lax.Precision.HIGHEST)
    return (first_term - second_term) * scale_norm_factor

def reference(voltages, wiring, positions, directions, gains, delays):
    dft_table = filter_table()
    sample_frames = voltages.reshape(ANTENNA_INPUTS // 64, 64 * SPECTRUM_BATCHES * BATCH_SPECTRA, FRAME_SAMPLES)

    def fourier_transform(block_rows):
        return jnp.dot(block_rows, dft_table, preferred_element_type=jnp.float32).astype(jnp.bfloat16)
    spectrum_rows = lax.map(fourier_transform, sample_frames).reshape(ANTENNA_INPUTS, SPECTRUM_BATCHES * BATCH_SPECTRA, 2 * FREQ_CHANNELS)
    place_x = jnp.take(positions[0], wiring)
    place_y = jnp.take(positions[1], wiring)
    gains_slot = jnp.take(gains, wiring, axis=2)

    def per_channel(channel):
        gain_re = lax.dynamic_index_in_dim(gains_slot[0], channel, 0, keepdims=False)
        gain_im = lax.dynamic_index_in_dim(gains_slot[1], channel, 0, keepdims=False)
        weight_re, weight_im = beam_weights(channel, directions, place_x, place_y, gain_re, gain_im)
        input_re = lax.dynamic_index_in_dim(spectrum_rows, channel, 2, keepdims=False)
        input_im = lax.dynamic_index_in_dim(spectrum_rows, channel + FREQ_CHANNELS, 2, keepdims=False)
        beam_re = jnp.dot(weight_re, input_re, preferred_element_type=jnp.float32) - jnp.dot(weight_im, input_im, preferred_element_type=jnp.float32)
        beam_im = jnp.dot(weight_re, input_im, preferred_element_type=jnp.float32) + jnp.dot(weight_im, input_re, preferred_element_type=jnp.float32)
        beam_power = (beam_re * beam_re + beam_im * beam_im).reshape(BEAMS, TB, AVG).mean(axis=2)
        return beam_power.astype(jnp.bfloat16)
    powers = lax.map(per_channel, jnp.arange(FREQ_CHANNELS, dtype=jnp.int32))
    series = powers.astype(jnp.float32)
    bin_ids = jnp.arange(TB, dtype=jnp.int32)
    turn_ids = bin_ids[:, None] * bin_ids[None, :] % TB
    phase_angle = two_pi / TB * turn_ids.astype(jnp.float32)
    spec_re = jnp.einsum('cbt,tk->kcb', series, jnp.cos(phase_angle), precision=lax.Precision.HIGHEST)
    spec_im = -jnp.einsum('cbt,tk->kcb', series, jnp.sin(phase_angle), precision=lax.Precision.HIGHEST)

    def per_freq(inputs):
        freq_id, part_re, part_im = inputs
        shift_angle = two_pi / TB * (freq_id * delays % TB).astype(jnp.float32)
        shift_re = jnp.cos(shift_angle)
        shift_im = jnp.sin(shift_angle)
        out_re = jnp.einsum('cd,cb->db', shift_re, part_re, precision=lax.Precision.HIGHEST) - jnp.einsum('cd,cb->db', shift_im, part_im, precision=lax.Precision.HIGHEST)
        out_im = jnp.einsum('cd,cb->db', shift_re, part_im, precision=lax.Precision.HIGHEST) + jnp.einsum('cd,cb->db', shift_im, part_re, precision=lax.Precision.HIGHEST)
        return (out_re, out_im)
    freq_re, freq_im = lax.map(per_freq, (bin_ids, spec_re, spec_im))
    return inverse_series(freq_re, freq_im)
```

```python
import functools
import math

import jax
import jax.numpy as jnp
import numpy as np
from jax import lax
from jax.experimental import pallas as pl
from jax.experimental.pallas import tpu as pltpu
from jax.sharding import PartitionSpec as P

AVG = 4
TB = 32
LOCAL_ANTENNAS = 4
SPECTRA = 128
LANES = 128
ROWS = 64
MESH = pl.DeviceIdType.MESH
F32 = jnp.float32
BF16 = jnp.bfloat16

NT = (((1,), (1,)), ((), ()))
TN = (((0,), (0,)), ((), ()))
NN = (((1,), (0,)), ((), ()))


def half_angle_coefficients():
    nodes = np.cos((np.arange(400) + 0.5) * np.pi / 400) * 0.125 + 0.125
    root = np.sqrt(nodes)
    sine = np.polynomial.chebyshev.Chebyshev.fit(
        nodes, np.sin(np.pi * root) / root, 4, domain=[0, 0.25]
    ).convert(kind=np.polynomial.Polynomial)
    cosine = np.polynomial.chebyshev.Chebyshev.fit(
        nodes, np.cos(np.pi * root), 5, domain=[0, 0.25]
    ).convert(kind=np.polynomial.Polynomial)
    return [float(x) for x in sine.coef], [float(x) for x in cosine.coef]


def filter_rows(channels, n_c, n_y):
    frame = 2 * channels
    sample = np.arange(frame)
    window = 0.5 - 0.5 * np.cos(2 * np.pi / frame * sample)
    channel = (np.arange(n_c)[None, :] * n_y + np.arange(n_y)[:, None]).reshape(-1)
    angle = 2 * np.pi / frame * (channel[:, None] * sample[None, :] % frame)
    scale = 1.0 / math.sqrt(3.0 * frame / 8.0)
    table = np.concatenate([np.cos(angle), -np.sin(angle)], axis=0) * window[None, :] * scale
    return jnp.asarray(table.astype(np.float32)).astype(BF16)


def dot(a, b, dims):
    return lax.dot_general(a, b, dims, preferred_element_type=F32)


def rotate(x, k):
    axis = x.ndim - 1
    width = x.shape[axis]
    t = lax.broadcasted_iota(jnp.int32, x.shape, axis) % TB
    near = pltpu.roll(x, width - k, axis)
    far = pltpu.roll(x, TB - k, axis)
    return jnp.where(t < TB - k, near, far)


def kernel(
    n_c,
    n_y,
    volt_ref,
    filt_ref,
    wiring_ref,
    pos_ref,
    dir_ref,
    gains_ref,
    delays_ref,
    out_ref,
    spec_ref,
    got_ref,
    turn_ref,
    col_ref,
    tab_ref,
    dirs_ref,
    wre_ref,
    wim_ref,
    give_ref,
    take_ref,
    piece_ref,
    part_ref,
    pow_ref,
    dm_ref,
    hot_ref,
    y_send,
    y_recv,
    c_send,
    c_recv,
    x_send,
    x_recv,
    p_send,
    p_recv,
    g_send,
    g_recv,
    f_send,
    own_sem,
):
    c = lax.axis_index("crate")
    board = lax.axis_index("board")
    y = board // 2
    k = board % 2
    channels = n_c * n_y
    antennas = 8 * channels
    plane = 4 * channels
    beams = 16 * n_c
    half_beams = beams // 2
    half_c = n_c // 2
    partner = (c, 2 * y + 1 - k)

    barrier = pltpu.get_barrier_semaphore()

    def greet_y(i, carry):
        peer = lax.rem(y + i, n_y)
        pl.semaphore_signal(barrier, inc=1, device_id=(c, 2 * peer + k), device_id_type=MESH)
        return carry

    def greet_c(i, carry):
        peer = lax.rem(c + i, n_c)
        pl.semaphore_signal(barrier, inc=1, device_id=(peer, board), device_id_type=MESH)
        return carry

    lax.fori_loop(1, n_y, greet_y, 0)
    lax.fori_loop(1, n_c, greet_c, 0)
    pl.semaphore_signal(barrier, inc=1, device_id=partner, device_id_type=MESH)

    for a in range(LOCAL_ANTENNAS):
        for part in range(2):
            rows = dot(filt_ref[part * channels : (part + 1) * channels, :], volt_ref[a], NT)
            spec_ref[:, a, :, part * SPECTRA : (part + 1) * SPECTRA] = rows.astype(BF16).reshape(
                n_y, n_c, SPECTRA
            )

    pl.semaphore_wait(barrier, n_y + n_c - 1)

    def y_copy(to, source, slot):
        return pltpu.make_async_remote_copy(
            src_ref=spec_ref.at[to],
            dst_ref=got_ref.at[source],
            send_sem=y_send.at[slot],
            recv_sem=y_recv.at[source],
            device_id=(c, 2 * to + k),
            device_id_type=MESH,
        )

    def y_start(i, carry):
        y_copy(lax.rem(y + i, n_y), y, i).start()
        return carry

    lax.fori_loop(1, n_y, y_start, 0)
    own_y = pltpu.make_async_copy(spec_ref.at[y], got_ref.at[y], own_sem.at[0])
    own_y.start()

    lane = lax.broadcasted_iota(jnp.int32, (plane // LANES, LANES), 1)
    even = wiring_ref[pl.ds(0, plane // LANES, stride=2), :]
    odd = wiring_ref[pl.ds(1, plane // LANES, stride=2), :]
    pick = (8 * (lane // 4) + 4 * k + lane % 4) % LANES
    ids = jnp.where(
        lane < LANES // 2,
        jnp.take_along_axis(even, pick, axis=1, mode="promise_in_bounds"),
        jnp.take_along_axis(odd, pick, axis=1, mode="promise_in_bounds"),
    )
    group = ids // LANES
    within = ids % LANES
    channel = c * n_y + y
    per_turn = 1.0 + channel.astype(F32) / channels
    norm = 1.0 / math.sqrt(antennas)

    def look_up(row_of):
        found = jnp.zeros(ids.shape, F32)
        for h in range(antennas // LANES):
            row = jnp.broadcast_to(row_of(slice(h * LANES, (h + 1) * LANES)), ids.shape)
            got = jnp.take_along_axis(row, within, axis=1, mode="promise_in_bounds")
            found = jnp.where(group == h, got, found)
        return found

    tab_ref[0] = look_up(lambda s: pos_ref[0:1, s]) * per_turn
    tab_ref[1] = look_up(lambda s: pos_ref[1:2, s]) * per_turn
    own_row = lax.broadcasted_iota(jnp.int32, (n_y, LANES), 0) == y

    def gain_row(part, s):
        return jnp.sum(jnp.where(own_row, gains_ref[part, :, s], 0.0), axis=0, keepdims=True)

    g_re = look_up(lambda s: gain_row(0, s)) * norm
    g_im = look_up(lambda s: gain_row(1, s)) * norm
    tab_ref[2] = g_re
    tab_ref[3] = g_im
    tab_ref[4] = 2.0 * g_re
    tab_ref[5] = 2.0 * g_im
    for i in range(2):
        dirs_ref[i] = jnp.broadcast_to(dir_ref[i : i + 1, :], (LANES, beams)).T

    sine, cosine = half_angle_coefficients()
    blocks = beams // ROWS

    def weights_block(i, carry):
        r = i // blocks
        first = pl.multiple_of(lax.rem(i, blocks) * ROWS, ROWS)
        columns = pl.ds(pl.multiple_of(r * LANES, LANES), LANES)
        px, py, gr, gi, gr2, gi2 = [tab_ref[n, pl.ds(r, 1), :] for n in range(6)]
        turns = dirs_ref[0, pl.ds(first, ROWS), :] * px + dirs_ref[1, pl.ds(first, ROWS), :] * py
        turn = turns - jnp.round(turns)
        square = turn * turn
        s = sine[-1]
        for coefficient in sine[-2::-1]:
            s = s * square + coefficient
        s = s * turn
        q = cosine[-1]
        for coefficient in cosine[-2::-1]:
            q = q * square + coefficient
        wre_ref[pl.ds(first, ROWS), columns] = (gr + s * (gi2 * q - gr2 * s)).astype(BF16)
        wim_ref[pl.ds(first, ROWS), columns] = (gi - s * (gi2 * s + gr2 * q)).astype(BF16)
        return carry

    steps = plane // LANES * blocks
    lax.fori_loop(0, steps // 2, weights_block, 0)

    own_y.wait()

    def y_wait(i, carry):
        source = lax.rem(y + n_y - i, n_y)
        y_copy(source, source, i).wait_recv()
        return carry

    lax.fori_loop(1, n_y, y_wait, 0)

    received = got_ref[...].reshape(n_y * LOCAL_ANTENNAS, n_c, 2 * SPECTRA)
    turn_ref[...] = jnp.swapaxes(received, 0, 1)

    def c_copy(to, source, slot):
        return pltpu.make_async_remote_copy(
            src_ref=turn_ref.at[to],
            dst_ref=col_ref.at[source],
            send_sem=c_send.at[slot],
            recv_sem=c_recv.at[source],
            device_id=(to, board),
            device_id_type=MESH,
        )

    def c_start(i, carry):
        c_copy(lax.rem(c + i, n_c), c, i).start()
        return carry

    lax.fori_loop(1, n_c, c_start, 0)
    own_c = pltpu.make_async_copy(turn_ref.at[c], col_ref.at[c], own_sem.at[1])
    own_c.start()

    lax.fori_loop(steps // 2, steps, weights_block, 0)

    offset = pl.multiple_of(board // 4 * LANES, LANES)
    values = delays_ref[:, pl.ds(offset, LANES)].astype(F32).astype(BF16)
    source = lax.broadcasted_iota(jnp.int32, (channels, channels), 0)
    place = lax.broadcasted_iota(jnp.int32, (channels, channels), 1)
    moved = (source == place % n_c * n_y + place // n_c).astype(F32).astype(BF16)
    dm_ref[...] = dot(values, moved, TN)
    mine = dm_ref[pl.ds(pl.multiple_of(board % 4 * TB, TB), TB), :]
    for d in range(TB):
        hot_ref[d * TB : (d + 1) * TB, :] = (mine == float(d)).astype(F32).astype(BF16)

    own_c.wait()

    def c_wait(i, carry):
        source = lax.rem(c + n_c - i, n_c)
        c_copy(source, source, i).wait_recv()
        return carry

    lax.fori_loop(1, n_c, c_wait, 0)

    columns = col_ref[...].reshape(plane, 2 * SPECTRA)

    def beams_of(which):
        rows = pl.ds(pl.multiple_of(which * half_beams, half_beams), half_beams)
        with_re = dot(wre_ref[rows, :], columns, NN)
        with_im = dot(wim_ref[rows, :], columns, NN)
        return (
            with_re[:, :SPECTRA] - with_im[:, SPECTRA:],
            with_re[:, SPECTRA:] + with_im[:, :SPECTRA],
        )

    give_re, give_im = beams_of(1 - k)
    give_ref[0] = give_re
    give_ref[1] = give_im
    swap = pltpu.make_async_remote_copy(
        src_ref=give_ref,
        dst_ref=take_ref,
        send_sem=x_send,
        recv_sem=x_recv,
        device_id=partner,
        device_id_type=MESH,
    )
    swap.start()
    keep_re, keep_im = beams_of(k)
    swap.wait_recv()
    beam_re = keep_re + take_ref[0]
    beam_im = keep_im + take_ref[1]
    energy = beam_re * beam_re + beam_im * beam_im

    high = energy.astype(BF16)
    low = (energy - high.astype(F32)).astype(BF16)
    from_s = lax.broadcasted_iota(jnp.int32, (SPECTRA, LANES), 0)
    to_t = lax.broadcasted_iota(jnp.int32, (SPECTRA, LANES), 1)
    mean = jnp.where(from_s // AVG == to_t % TB, 1.0 / AVG, 0.0).astype(BF16)
    power = dot(high, mean, NN) + dot(low, mean, NN)
    beam = lax.broadcasted_iota(jnp.int32, (half_beams, LANES), 0)
    slot = lax.broadcasted_iota(jnp.int32, (half_beams, LANES), 1)
    power = jnp.where(beam % 4 == slot // TB, power, 0.0).astype(BF16)
    to_row = lax.broadcasted_iota(jnp.int32, (8 * half_c, half_beams), 0)
    of_beam = lax.broadcasted_iota(jnp.int32, (8 * half_c, half_beams), 1)
    gather = (of_beam // 16 == to_row // 8) & (of_beam % 16 // 4 == to_row % 8)
    piece_ref[...] = dot(gather.astype(F32).astype(BF16), power, NN).reshape(half_c, 8, LANES)

    def p_copy(index, source, to):
        return pltpu.make_async_remote_copy(
            src_ref=piece_ref.at[index],
            dst_ref=part_ref.at[source],
            send_sem=p_send.at[index],
            recv_sem=p_recv.at[source],
            device_id=(to, board),
            device_id_type=MESH,
        )

    def p_start(i, carry):
        to = k * half_c + i

        @pl.when(to != c)
        def _():
            p_copy(i, c, to).start()

        return carry

    lax.fori_loop(0, half_c, p_start, 0)
    holds = c // half_c == k

    def g_copy(to, source, sem, device):
        return pltpu.make_async_remote_copy(
            src_ref=pow_ref.at[source],
            dst_ref=pow_ref.at[source],
            send_sem=sem.at[to],
            recv_sem=g_recv.at[source],
            device_id=device,
            device_id_type=MESH,
        )

    @pl.when(holds)
    def _():
        own_p = pltpu.make_async_copy(
            piece_ref.at[lax.rem(c, half_c)], part_ref.at[c], own_sem.at[2]
        )
        own_p.start()
        own_p.wait()

        def p_wait(i, carry):
            source = lax.rem(c + i, n_c)
            p_copy(0, source, source).wait_recv()
            return carry

        lax.fori_loop(1, n_c, p_wait, 0)
        for j in range(4):
            pow_ref[y, :, j * LANES : (j + 1) * LANES] = part_ref[:, j, :].astype(BF16)

        def g_start(i, carry):
            to = lax.rem(y + i, n_y)
            g_copy(to, y, g_send, (c, 2 * to + k)).start()
            return carry

        lax.fori_loop(1, n_y, g_start, 0)
        g_copy(y, y, f_send, partner).start()

        def g_wait(i, carry):
            source = lax.rem(y + n_y - i, n_y)
            g_copy(source, source, g_send, (c, 2 * source + k)).wait_recv()
            g_copy(source, source, f_send, partner).start()
            return carry

        lax.fori_loop(1, n_y, g_wait, 0)

    @pl.when(jnp.logical_not(holds))
    def _():
        def f_wait(i, carry):
            g_copy(i, i, f_send, partner).wait_recv()
            return carry

        lax.fori_loop(0, n_y, f_wait, 0)

    for j in range(4):
        series = pow_ref[:, :, j * LANES : (j + 1) * LANES].reshape(channels, LANES)
        total = dot(hot_ref[...], series, NN)
        step = TB // 2
        while step:
            rows = step * TB
            total = total[:rows] + rotate(total[rows:], step)
            step //= 2
        mean_of = total
        step = TB // 2
        while step:
            mean_of = mean_of + rotate(mean_of, step)
            step //= 2
        result = (total - mean_of * (1.0 / TB)) * (1.0 / math.sqrt(channels))
        for q in range(4):
            out_ref[4 * j + q] = result[:, q * TB : (q + 1) * TB]

    def y_sent(i, carry):
        y_copy(lax.rem(y + i, n_y), y, i).wait_send()
        return carry

    lax.fori_loop(1, n_y, y_sent, 0)

    def c_sent(i, carry):
        c_copy(lax.rem(c + i, n_c), c, i).wait_send()
        return carry

    lax.fori_loop(1, n_c, c_sent, 0)
    swap.wait_send()

    def p_sent(i, carry):
        to = k * half_c + i

        @pl.when(to != c)
        def _():
            p_copy(i, c, to).wait_send()

        return carry

    lax.fori_loop(0, half_c, p_sent, 0)

    @pl.when(holds)
    def _():
        def g_sent(i, carry):
            to = lax.rem(y + i, n_y)
            g_copy(to, y, g_send, (c, 2 * to + k)).wait_send()
            g_copy(to, to, f_send, partner).wait_send()
            return carry

        lax.fori_loop(1, n_y, g_sent, 0)
        g_copy(y, y, f_send, partner).wait_send()


def shards(n_c, n_y, voltages, wiring, positions, directions, gains, delays):
    channels = n_c * n_y
    frame = 2 * channels
    plane = 4 * channels
    beams = 16 * n_c
    half_beams = beams // 2
    frames = voltages.reshape(LOCAL_ANTENNAS, SPECTRA, frame)
    table = filter_rows(channels, n_c, n_y)
    ids = wiring.reshape(-1, LANES)
    dma = pltpu.SemaphoreType.DMA
    vmem = pl.BlockSpec(memory_space=pltpu.VMEM)
    return pl.pallas_call(
        functools.partial(kernel, n_c, n_y),
        out_shape=jax.ShapeDtypeStruct((16, TB, TB), F32),
        in_specs=[vmem] * 7,
        out_specs=vmem,
        scratch_shapes=[
            pltpu.VMEM((n_y, LOCAL_ANTENNAS, n_c, 2 * SPECTRA), BF16),
            pltpu.VMEM((n_y, LOCAL_ANTENNAS, n_c, 2 * SPECTRA), BF16),
            pltpu.VMEM((n_c, LOCAL_ANTENNAS * n_y, 2 * SPECTRA), BF16),
            pltpu.VMEM((n_c, LOCAL_ANTENNAS * n_y, 2 * SPECTRA), BF16),
            pltpu.VMEM((6, plane // LANES, LANES), F32),
            pltpu.VMEM((2, beams, LANES), F32),
            pltpu.VMEM((beams, plane), BF16),
            pltpu.VMEM((beams, plane), BF16),
            pltpu.VMEM((2, half_beams, SPECTRA), F32),
            pltpu.VMEM((2, half_beams, SPECTRA), F32),
            pltpu.VMEM((n_c // 2, 8, LANES), F32),
            pltpu.VMEM((n_c, 8, LANES), F32),
            pltpu.VMEM((n_y, n_c, 4 * LANES), BF16),
            pltpu.VMEM((LANES, channels), F32),
            pltpu.VMEM((TB * TB, channels), BF16),
            dma((n_y,)),
            dma((n_y,)),
            dma((n_c,)),
            dma((n_c,)),
            dma,
            dma,
            dma((n_c // 2,)),
            dma((n_c,)),
            dma((n_y,)),
            dma((n_y,)),
            dma((n_y,)),
            dma((3,)),
        ],
        compiler_params=pltpu.CompilerParams(
            collective_id=0, has_side_effects=True, vmem_limit_bytes=60 * 1024 * 1024
        ),
    )(frames, table, ids, positions, directions, gains, delays)


def solution(mesh):
    n_c = mesh.shape["crate"]
    n_y = mesh.shape["board"] // 2
    in_specs = (P(("crate", "board"), None), P(), P(), P(), P(None, "crate", None), P())
    return jax.shard_map(
        functools.partial(shards, n_c, n_y),
        mesh=mesh,
        in_specs=in_specs,
        out_specs=P("crate", "board", None),
        check_vma=False,
    )
```

```python
import functools
import math

import jax
import jax.numpy as jnp
import numpy as np
from jax import lax
from jax.experimental import pallas as pl
from jax.experimental.pallas import tpu as pltpu
from jax.sharding import PartitionSpec as P

AVG = 4
TB = 32
LOCAL_ANTENNAS = 4
SPECTRA = 128
LANES = 128
ROWS = 64
MESH = pl.DeviceIdType.MESH
F32 = jnp.float32
BF16 = jnp.bfloat16

NT = (((1,), (1,)), ((), ()))
TN = (((0,), (0,)), ((), ()))
NN = (((1,), (0,)), ((), ()))


def half_angle_coefficients():
    nodes = np.cos((np.arange(400) + 0.5) * np.pi / 400) * 0.125 + 0.125
    root = np.sqrt(nodes)
    sine = np.polynomial.chebyshev.Chebyshev.fit(
        nodes, np.sin(np.pi * root) / root, 4, domain=[0, 0.25]
    ).convert(kind=np.polynomial.Polynomial)
    cosine = np.polynomial.chebyshev.Chebyshev.fit(
        nodes, np.cos(np.pi * root), 5, domain=[0, 0.25]
    ).convert(kind=np.polynomial.Polynomial)
    return [float(x) for x in sine.coef], [float(x) for x in cosine.coef]


def filter_rows(channels, n_c, n_y):
    frame = 2 * channels
    sample = np.arange(frame)
    window = 0.5 - 0.5 * np.cos(2 * np.pi / frame * sample)
    channel = (np.arange(n_c)[None, :] * n_y + np.arange(n_y)[:, None]).reshape(-1)
    angle = 2 * np.pi / frame * (channel[:, None] * sample[None, :] % frame)
    scale = 1.0 / math.sqrt(3.0 * frame / 8.0)
    table = np.concatenate([np.cos(angle), -np.sin(angle)], axis=0) * window[None, :] * scale
    return jnp.asarray(table.astype(np.float32)).astype(BF16)


def dot(a, b, dims):
    return lax.dot_general(a, b, dims, preferred_element_type=F32)


def rotate(x, k):
    lane = lax.broadcasted_iota(jnp.int32, x.shape, x.ndim - 1)
    return jnp.take_along_axis(
        x, lane // TB * TB + (lane + k) % TB, axis=x.ndim - 1, mode="promise_in_bounds"
    )


def kernel(
    n_c,
    n_y,
    volt_hbm,
    filt_hbm,
    wiring_hbm,
    pos_hbm,
    dir_hbm,
    gains_hbm,
    delays_hbm,
    out_ref,
    volt_ref,
    filt_ref,
    wiring_ref,
    pos_ref,
    dir_ref,
    gains_ref,
    delays_ref,
    a_spec,
    a_got,
    a_turn,
    b_spec,
    b_got,
    b_turn,
    col_ref,
    tab_ref,
    dirs_ref,
    wre_ref,
    wim_ref,
    give_ref,
    take_ref,
    piece_ref,
    pow_ref,
    dm_ref,
    hot_ref,
    in_sem,
    ay_send,
    ay_recv,
    ac_send,
    ac_recv,
    by_send,
    by_recv,
    bc_send,
    bc_recv,
    x_send,
    x_recv,
    p_send,
    p_recv,
    f_send,
    own_sem,
):
    c = lax.axis_index("crate")
    board = lax.axis_index("board")
    y = board // 2
    k = board % 2
    channels = n_c * n_y
    antennas = 8 * channels
    plane = 4 * channels
    beams = 16 * n_c
    half_beams = beams // 2
    half_c = n_c // 2
    partner = (c, 2 * y + 1 - k)

    offset = pl.multiple_of(board // 4 * LANES, LANES)
    pairs = [
        (volt_hbm, volt_ref),
        (filt_hbm, filt_ref),
        (wiring_hbm, wiring_ref),
        (pos_hbm, pos_ref),
        (dir_hbm, dir_ref),
        (gains_hbm, gains_ref),
        (delays_hbm.at[:, pl.ds(offset, LANES)], delays_ref),
    ]
    loads = [pltpu.make_async_copy(*pair, in_sem.at[i]) for i, pair in enumerate(pairs)]
    for load in loads:
        load.start()

    barrier = pltpu.get_barrier_semaphore()

    def greet_y(i, carry):
        peer = lax.rem(y + i, n_y)
        pl.semaphore_signal(barrier, inc=1, device_id=(c, 2 * peer + k), device_id_type=MESH)
        return carry

    def greet_c(i, carry):
        peer = lax.rem(c + i, n_c)
        pl.semaphore_signal(barrier, inc=1, device_id=(peer, board), device_id_type=MESH)
        return carry

    lax.fori_loop(1, n_c, greet_c, 0)
    lax.fori_loop(1, n_y, greet_y, 0)
    pl.semaphore_signal(barrier, inc=1, device_id=partner, device_id_type=MESH)

    loads[0].wait()
    loads[1].wait()
    turned = jnp.swapaxes(volt_ref[...], 0, 1)
    frame_rows = turned.shape[0] // LOCAL_ANTENNAS

    def spectra(antenna, part):
        samples = jnp.concatenate(
            [turned[LOCAL_ANTENNAS * q + antenna] for q in range(frame_rows)], axis=1
        )
        rows = dot(filt_ref[part * channels : (part + 1) * channels, :], samples, NT)
        return rows.reshape(n_y, n_c, SPECTRA)

    for part in range(2):
        lanes = slice(part * SPECTRA, (part + 1) * SPECTRA)
        both = jnp.concatenate([spectra(2, part), spectra(3, part)], axis=0)
        b_spec[:, :, lanes] = jnp.swapaxes(both, 0, 1).astype(BF16)

    def copy(src, dst, send, recv, device):
        return pltpu.make_async_remote_copy(
            src_ref=src,
            dst_ref=dst,
            send_sem=send,
            recv_sem=recv,
            device_id=device,
            device_id_type=MESH,
        )

    def over_y(src, dst, send, recv):
        def one(to, source, slot):
            device = (c, 2 * to + k)
            return copy(src(to), dst(source), send.at[slot], recv.at[source], device)

        def start(i, carry):
            one(lax.rem(y + i, n_y), y, i).start()
            return carry

        def arrive(i, carry):
            source = lax.rem(y + n_y - i, n_y)
            one(source, source, i).wait_recv()
            return carry

        def depart(i, carry):
            one(lax.rem(y + i, n_y), y, i).wait_send()
            return carry

        return [lambda f=f: lax.fori_loop(1, n_y, f, 0) for f in (start, arrive, depart)]

    def over_c(src, dst, send, recv):
        def one(to, source, slot):
            return copy(src(to), dst(source), send.at[slot], recv.at[source], (to, board))

        def start(i, carry):
            one(lax.rem(c + i, n_c), c, i).start()
            return carry

        def arrive(i, carry):
            source = lax.rem(c + n_c - i, n_c)
            one(source, source, i).wait_recv()
            return carry

        def depart(i, carry):
            one(lax.rem(c + i, n_c), c, i).wait_send()
            return carry

        return [lambda f=f: lax.fori_loop(1, n_c, f, 0) for f in (start, arrive, depart)]

    def a_rows(source):
        return col_ref.at[pl.ds(pl.multiple_of(source * 2 * n_y, 2 * n_y), 2 * n_y)]

    def b_rows(source):
        first = pl.multiple_of(plane // 2 + source * 2 * n_c, 2 * n_c)
        return col_ref.at[pl.ds(first, 2 * n_c)]

    a_one = over_y(lambda i: a_spec.at[i], lambda i: a_got.at[i], ay_send, ay_recv)
    a_two = over_c(lambda i: a_turn.at[i], a_rows, ac_send, ac_recv)
    b_one = over_c(lambda i: b_spec.at[i], lambda i: b_got.at[i], bc_send, bc_recv)
    b_two = over_y(lambda i: b_turn.at[i], b_rows, by_send, by_recv)

    pl.semaphore_wait(barrier, n_y + n_c - 1)
    b_one[0]()
    own_b = pltpu.make_async_copy(b_spec.at[c], b_got.at[c], own_sem.at[0])
    own_b.start()
    for antenna in range(2):
        for part in range(2):
            lanes = slice(part * SPECTRA, (part + 1) * SPECTRA)
            a_spec[:, antenna, :, lanes] = spectra(antenna, part).astype(BF16)
    a_one[0]()
    own_a = pltpu.make_async_copy(a_spec.at[y], a_got.at[y], own_sem.at[1])
    own_a.start()

    for load in loads[2:]:
        load.wait()
    shape = (plane // LANES, LANES)
    place = lax.broadcasted_iota(jnp.int32, shape, 0) * LANES
    place = place + lax.broadcasted_iota(jnp.int32, shape, 1)
    in_b = place - plane // 2
    of_a = (place // (2 * n_y) * 2 * n_y + place % (2 * n_y) // 2 * 2 + k) * 4 + place % 2
    of_b = (in_b % n_c * 2 * n_y + in_b // (2 * n_c) * 2 + k) * 4 + 2 + in_b // n_c % 2
    row_id = jnp.where(place < plane // 2, of_a, of_b)

    def look_up(index, row_of, dtype):
        group = index // LANES
        within = index % LANES
        found = jnp.zeros(shape, dtype)
        for h in range(antennas // LANES):
            row = jnp.broadcast_to(row_of(h), shape)
            got = jnp.take_along_axis(row, within, axis=1, mode="promise_in_bounds")
            found = jnp.where(group == h, got, found)
        return found

    def part_of(h):
        return slice(h * LANES, (h + 1) * LANES)

    ids = look_up(row_id, lambda h: wiring_ref[h : h + 1, :], jnp.int32)
    channel = c * n_y + y
    per_turn = 1.0 + channel.astype(F32) / channels
    norm = 1.0 / math.sqrt(antennas)
    own_row = lax.broadcasted_iota(jnp.int32, (n_y, LANES), 0) == y

    def gain_row(part, h):
        rows = gains_ref[part, :, part_of(h)]
        return jnp.sum(jnp.where(own_row, rows, 0.0), axis=0, keepdims=True)

    tab_ref[0] = look_up(ids, lambda h: pos_ref[0:1, part_of(h)], F32) * per_turn
    tab_ref[1] = look_up(ids, lambda h: pos_ref[1:2, part_of(h)], F32) * per_turn
    g_re = look_up(ids, lambda h: gain_row(0, h), F32) * norm
    g_im = look_up(ids, lambda h: gain_row(1, h), F32) * norm
    tab_ref[2] = g_re
    tab_ref[3] = g_im
    tab_ref[4] = 2.0 * g_re
    tab_ref[5] = 2.0 * g_im
    for i in range(2):
        dirs_ref[i] = jnp.broadcast_to(dir_ref[i : i + 1, :], (LANES, beams)).T

    sine, cosine = half_angle_coefficients()
    blocks = beams // ROWS

    def weights_block(i, carry):
        r = i // blocks
        first = pl.multiple_of(lax.rem(i, blocks) * ROWS, ROWS)
        columns = pl.ds(pl.multiple_of(r * LANES, LANES), LANES)
        px, py, gr, gi, gr2, gi2 = [tab_ref[n, pl.ds(r, 1), :] for n in range(6)]
        turns = dirs_ref[0, pl.ds(first, ROWS), :] * px + dirs_ref[1, pl.ds(first, ROWS), :] * py
        turn = turns - jnp.round(turns)
        square = turn * turn
        s = sine[-1]
        for coefficient in sine[-2::-1]:
            s = s * square + coefficient
        s = s * turn
        q = cosine[-1]
        for coefficient in cosine[-2::-1]:
            q = q * square + coefficient
        wre_ref[pl.ds(first, ROWS), columns] = (gr + s * (gi2 * q - gr2 * s)).astype(BF16)
        wim_ref[pl.ds(first, ROWS), columns] = (gi - s * (gi2 * s + gr2 * q)).astype(BF16)
        return carry

    steps = plane // LANES * blocks
    lax.fori_loop(0, steps // 2, weights_block, 0)

    own_a.wait()
    a_one[1]()
    received = a_got[...].reshape(2 * n_y, n_c, 2 * SPECTRA)
    a_turn[...] = jnp.swapaxes(received, 0, 1)
    a_two[0]()
    own_a = pltpu.make_async_copy(a_turn.at[c], a_rows(c), own_sem.at[2])
    own_a.start()

    own_b.wait()
    b_one[1]()
    received = jnp.swapaxes(b_got[...], 0, 1)
    for antenna in range(2):
        b_turn[:, antenna * n_c : (antenna + 1) * n_c, :] = received[
            antenna * n_y : (antenna + 1) * n_y
        ]
    b_two[0]()
    own_b = pltpu.make_async_copy(b_turn.at[y], b_rows(y), own_sem.at[3])
    own_b.start()

    lax.fori_loop(steps // 2, steps, weights_block, 0)

    values = delays_ref[...].astype(F32).astype(BF16)
    source = lax.broadcasted_iota(jnp.int32, (channels, channels), 0)
    position = lax.broadcasted_iota(jnp.int32, (channels, channels), 1)
    tiles = channels // 4
    piece = position % tiles * 4 + position // tiles
    moved = (source == piece % n_c * n_y + piece // n_c).astype(F32).astype(BF16)
    dm_ref[...] = dot(values, moved, TN)
    mine = dm_ref[pl.ds(pl.multiple_of(board % 4 * TB, TB), TB), :]
    for d in range(TB):
        hot_ref[d * TB : (d + 1) * TB, :] = (mine == float(d)).astype(F32).astype(BF16)

    own_a.wait()
    own_b.wait()
    a_two[1]()
    b_two[1]()

    def beams_of(which):
        rows = pl.ds(pl.multiple_of(which * half_beams, half_beams), half_beams)
        with_re = dot(wre_ref[rows, :], col_ref[...], NN)
        with_im = dot(wim_ref[rows, :], col_ref[...], NN)
        return (
            with_re[:, :SPECTRA] - with_im[:, SPECTRA:],
            with_re[:, SPECTRA:] + with_im[:, :SPECTRA],
        )

    give_re, give_im = beams_of(1 - k)
    give_ref[0] = give_re
    give_ref[1] = give_im
    swap = copy(give_ref, take_ref, x_send, x_recv, partner)
    swap.start()
    keep_re, keep_im = beams_of(k)
    swap.wait_recv()
    beam_re = keep_re + take_ref[0]
    beam_im = keep_im + take_ref[1]
    energy = beam_re * beam_re + beam_im * beam_im

    high = energy.astype(BF16)
    low = (energy - high.astype(F32)).astype(BF16)
    from_s = lax.broadcasted_iota(jnp.int32, (SPECTRA, LANES), 0)
    to_t = lax.broadcasted_iota(jnp.int32, (SPECTRA, LANES), 1)
    mean = jnp.where(from_s // AVG == to_t % TB, 1.0 / AVG, 0.0).astype(BF16)
    power = dot(high, mean, NN) + dot(low, mean, NN)
    beam = lax.broadcasted_iota(jnp.int32, (half_beams, LANES), 0)
    slot = lax.broadcasted_iota(jnp.int32, (half_beams, LANES), 1)
    power = jnp.where(beam % 4 == slot // TB, power, 0.0).astype(BF16)
    to_row = lax.broadcasted_iota(jnp.int32, (half_beams // 4, half_beams), 0)
    of_beam = lax.broadcasted_iota(jnp.int32, (half_beams // 4, half_beams), 1)
    gather = (of_beam // 4 == to_row).astype(F32).astype(BF16)
    piece_ref[...] = dot(gather, power, NN).reshape(half_c, 4, LANES).astype(BF16)

    holds = c // half_c == k
    count = half_c * n_y
    mine_at = y * n_c + c

    def p_copy(i):
        return copy(
            piece_ref.at[i // n_y],
            pow_ref.at[mine_at],
            p_send,
            p_recv.at[y],
            (k * half_c + i // n_y, 2 * lax.rem(i, n_y) + k),
        )

    def p_start(i, carry):
        away = (k * half_c + i // n_y != c) | (lax.rem(i, n_y) != y)

        @pl.when(away)
        def _():
            p_copy(i).start()

        return carry

    lax.fori_loop(0, count, p_start, 0)

    def group(source, size):
        return pow_ref.at[pl.ds(pl.multiple_of(source * n_c, n_c), size)]

    def forward(source):
        rows = group(source, n_c)
        return copy(rows, rows, f_send.at[source], p_recv.at[source], partner)

    def group_wait(source, size):
        rows = group(source, size)
        copy(rows, rows, p_send, p_recv.at[source], partner).wait_recv()

    @pl.when(holds)
    def _():
        own_p = pltpu.make_async_copy(
            piece_ref.at[lax.rem(c, half_c)], pow_ref.at[mine_at], own_sem.at[4]
        )
        own_p.start()
        own_p.wait()
        group_wait(y, n_c - 1)
        forward(y).start()

        def g_wait(i, carry):
            source = lax.rem(y + i, n_y)
            group_wait(source, n_c)
            forward(source).start()
            return carry

        lax.fori_loop(1, n_y, g_wait, 0)

    @pl.when(jnp.logical_not(holds))
    def _():
        def f_wait(i, carry):
            forward(i).wait_recv()
            return carry

        lax.fori_loop(0, n_y, f_wait, 0)

    series = jnp.swapaxes(pow_ref[...].reshape(tiles, 16, LANES), 0, 1)
    for pair in range(2):
        both = [
            jnp.concatenate([series[4 * r + 2 * pair + j] for r in range(4)], axis=0)
            for j in range(2)
        ]
        sums = dot(hot_ref[...], jnp.concatenate(both, axis=1), NN)
        for j in range(2):
            total = sums[:, j * LANES : (j + 1) * LANES]
            step = TB // 2
            while step:
                rows = step * TB
                total = total[:rows] + rotate(total[rows:], step)
                step //= 2
            mean_of = total
            step = TB // 2
            while step:
                mean_of = mean_of + rotate(mean_of, step)
                step //= 2
            result = (total - mean_of * (1.0 / TB)) * (1.0 / math.sqrt(channels))
            for q in range(4):
                out_ref[4 * (2 * pair + j) + q] = result[:, q * TB : (q + 1) * TB]

    for exchange in (b_one, a_one, a_two, b_two):
        exchange[2]()
    swap.wait_send()

    @pl.when(holds)
    def _():
        rows = pow_ref.at[pl.ds(0, count - 1)]
        copy(rows, rows, p_send, p_recv.at[0], partner).wait_send()

        def f_sent(i, carry):
            forward(i).wait_send()
            return carry

        lax.fori_loop(0, n_y, f_sent, 0)

    @pl.when(jnp.logical_not(holds))
    def _():
        rows = pow_ref.at[pl.ds(0, count)]
        copy(rows, rows, p_send, p_recv.at[0], partner).wait_send()


def shards(n_c, n_y, voltages, wiring, positions, directions, gains, delays):
    channels = n_c * n_y
    frame = 2 * channels
    plane = 4 * channels
    beams = 16 * n_c
    half_beams = beams // 2
    samples = voltages.reshape(LOCAL_ANTENNAS, SPECTRA * frame // LANES, LANES).transpose(1, 0, 2)
    samples = samples.reshape(SPECTRA, frame // LANES * LOCAL_ANTENNAS, LANES)
    table = filter_rows(channels, n_c, n_y)
    ids = wiring.reshape(-1, LANES)
    operands = (samples, table, ids, positions, directions, gains, delays)
    loaded = [pltpu.VMEM(x.shape, x.dtype) for x in operands[:-1]]
    loaded.append(pltpu.VMEM((channels, LANES), delays.dtype))
    dma = pltpu.SemaphoreType.DMA
    by_y = pltpu.VMEM((n_y, 2, n_c, 2 * SPECTRA), BF16)
    by_c = pltpu.VMEM((n_c, 2 * n_y, 2 * SPECTRA), BF16)
    return pl.pallas_call(
        functools.partial(kernel, n_c, n_y),
        out_shape=jax.ShapeDtypeStruct((16, TB, TB), F32),
        in_specs=[pl.BlockSpec(memory_space=pl.ANY)] * len(operands),
        out_specs=pl.BlockSpec(memory_space=pltpu.VMEM),
        scratch_shapes=[
            *loaded,
            by_y,
            by_y,
            by_c,
            by_c,
            by_c,
            pltpu.VMEM((n_y, 2 * n_c, 2 * SPECTRA), BF16),
            pltpu.VMEM((plane, 2 * SPECTRA), BF16),
            pltpu.VMEM((6, plane // LANES, LANES), F32),
            pltpu.VMEM((2, beams, LANES), F32),
            pltpu.VMEM((beams, plane), BF16),
            pltpu.VMEM((beams, plane), BF16),
            pltpu.VMEM((2, half_beams, SPECTRA), F32),
            pltpu.VMEM((2, half_beams, SPECTRA), F32),
            pltpu.VMEM((n_c // 2, 4, LANES), BF16),
            pltpu.VMEM((channels, 4, LANES), BF16),
            pltpu.VMEM((LANES, channels), F32),
            pltpu.VMEM((TB * TB, channels), BF16),
            dma((len(operands),)),
            dma((n_y,)),
            dma((n_y,)),
            dma((n_c,)),
            dma((n_c,)),
            dma((n_y,)),
            dma((n_y,)),
            dma((n_c,)),
            dma((n_c,)),
            dma,
            dma,
            dma,
            dma((n_y,)),
            dma((n_y,)),
            dma((5,)),
        ],
        compiler_params=pltpu.CompilerParams(
            collective_id=0, has_side_effects=True, vmem_limit_bytes=60 * 1024 * 1024
        ),
    )(*operands)


def solution(mesh):
    n_c = mesh.shape["crate"]
    n_y = mesh.shape["board"] // 2
    in_specs = (P(("crate", "board"), None), P(), P(), P(), P(None, "crate", None), P())
    return jax.shard_map(
        functools.partial(shards, n_c, n_y),
        mesh=mesh,
        in_specs=in_specs,
        out_specs=P("crate", "board", None),
        check_vma=False,
    )
```

```python
import functools
import math

import jax
import jax.numpy as jnp
import numpy as np
from jax import lax
from jax.experimental import pallas as pl
from jax.experimental.pallas import tpu as pltpu
from jax.sharding import PartitionSpec as P

AVG = 4
TB = 32
LOCAL_ANTENNAS = 4
SPECTRA = 128
LANES = 128
ROWS = 64
MESH = pl.DeviceIdType.MESH
F32 = jnp.float32
BF16 = jnp.bfloat16

NT = (((1,), (1,)), ((), ()))
TN = (((0,), (0,)), ((), ()))
NN = (((1,), (0,)), ((), ()))


def half_angle_coefficients():
    nodes = np.cos((np.arange(400) + 0.5) * np.pi / 400) * 0.125 + 0.125
    root = np.sqrt(nodes)
    sine = np.polynomial.chebyshev.Chebyshev.fit(
        nodes, np.sin(np.pi * root) / root, 4, domain=[0, 0.25]
    ).convert(kind=np.polynomial.Polynomial)
    cosine = np.polynomial.chebyshev.Chebyshev.fit(
        nodes, np.cos(np.pi * root), 5, domain=[0, 0.25]
    ).convert(kind=np.polynomial.Polynomial)
    return [float(x) for x in sine.coef], [float(x) for x in cosine.coef]


def filter_rows(channels, n_c, n_y):
    frame = 2 * channels
    sample = np.arange(frame)
    window = 0.5 - 0.5 * np.cos(2 * np.pi / frame * sample)
    channel = (np.arange(n_c)[None, :] * n_y + np.arange(n_y)[:, None]).reshape(-1)
    angle = 2 * np.pi / frame * (channel[:, None] * sample[None, :] % frame)
    scale = 1.0 / math.sqrt(3.0 * frame / 8.0)
    table = np.concatenate([np.cos(angle), -np.sin(angle)], axis=0) * window[None, :] * scale
    return jnp.asarray(table.astype(np.float32)).astype(BF16)


def far_first(size):
    return sorted(range(size), key=lambda d: -min(d, size - d))


def dot(a, b, dims):
    return lax.dot_general(a, b, dims, preferred_element_type=F32)


def rotate(x, k):
    lane = lax.broadcasted_iota(jnp.int32, x.shape, x.ndim - 1)
    return jnp.take_along_axis(
        x, lane // TB * TB + (lane + k) % TB, axis=x.ndim - 1, mode="promise_in_bounds"
    )


def kernel(
    n_c,
    n_y,
    volt_hbm,
    filt_hbm,
    wiring_hbm,
    pos_hbm,
    dir_hbm,
    gains_hbm,
    delays_hbm,
    out_hbm,
    volt_ref,
    filt_ref,
    wiring_ref,
    pos_ref,
    dir_ref,
    gains_ref,
    delays_ref,
    a_spec,
    a_got,
    a_turn,
    a_col,
    b_spec,
    b_got,
    b_turn,
    b_col,
    tab_ref,
    dirs_ref,
    wre_ref,
    wim_ref,
    give_ref,
    take_ref,
    piece_ref,
    pow_ref,
    dm_ref,
    hot_ref,
    made_ref,
    in_sem,
    a_send,
    a_recv,
    b_send,
    b_recv,
    x_send,
    x_recv,
    p_send,
    p_recv,
    f_send,
    own_sem,
    out_sem,
):
    c = lax.axis_index("crate")
    board = lax.axis_index("board")
    y = board // 2
    k = board % 2
    channels = n_c * n_y
    antennas = 8 * channels
    plane = 4 * channels
    beams = 16 * n_c
    half_beams = beams // 2
    half_c = n_c // 2
    partner = (c, 2 * y + 1 - k)
    n_x = min(8, n_c)
    n_z = n_c // n_x
    x = c % n_x
    z = c // n_x
    mine_at = y * n_c + c

    steps_c = [(dz, dx) for dz in range(n_z) for dx in range(n_x)]
    steps_c.sort(key=lambda s: -min(s[0], n_z - s[0]) - min(s[1], n_x - s[1]))
    crates = [(z + dz) % n_z * n_x + (x + dx) % n_x for dz, dx in steps_c[:-1]]
    places = [(y + dy) % n_y for dy in far_first(n_y)[:-1]]

    offset = pl.multiple_of(board // 4 * LANES, LANES)
    pairs = [
        (volt_hbm, volt_ref),
        (filt_hbm, filt_ref),
        (wiring_hbm, wiring_ref),
        (pos_hbm, pos_ref),
        (dir_hbm, dir_ref),
        (gains_hbm, gains_ref),
        (delays_hbm.at[:, pl.ds(offset, LANES)], delays_ref),
    ]
    loads = [pltpu.make_async_copy(*pair, in_sem.at[i]) for i, pair in enumerate(pairs)]
    for load in loads:
        load.start()

    barrier = pltpu.get_barrier_semaphore()
    for device in [(i, board) for i in crates] + [(c, 2 * i + k) for i in places] + [partner]:
        pl.semaphore_signal(barrier, inc=1, device_id=device, device_id_type=MESH)

    loads[0].wait()
    loads[1].wait()
    turned = jnp.swapaxes(volt_ref[...], 0, 1)
    frame_rows = turned.shape[0] // LOCAL_ANTENNAS
    for antenna in range(LOCAL_ANTENNAS):
        samples = jnp.concatenate(
            [turned[LOCAL_ANTENNAS * q + antenna] for q in range(frame_rows)], axis=1
        )
        rows = dot(filt_ref[...], samples, NT).reshape(2, n_y, n_c, SPECTRA)
        for part in range(2):
            lanes = slice(part * SPECTRA, (part + 1) * SPECTRA)
            if antenna < 2:
                a_spec[antenna, :, :, lanes] = rows[part].astype(BF16)
            else:
                b_spec[antenna - 2, :, :, lanes] = jnp.swapaxes(rows[part], 0, 1).astype(BF16)

    def copy(src, dst, send, recv, device):
        return pltpu.make_async_remote_copy(
            src_ref=src,
            dst_ref=dst,
            send_sem=send,
            recv_sem=recv,
            device_id=device,
            device_id_type=MESH,
        )

    class Exchange:
        def __init__(self, src, dst, send, recv, own_sem, along_y):
            self.refs = (src, dst)
            self.sems = (send, recv)
            self.here, self.others = (y, places) if along_y else (c, crates)
            self.device = (lambda i: (c, 2 * i + k)) if along_y else (lambda i: (i, board))
            own = (src.at[self.here], dst.at[self.here], own_sem)
            self.own = pltpu.make_async_copy(*own)
            count = pl.ds(0, len(self.others))
            self.all = copy(src.at[count], dst.at[count], send, recv, partner)

        def start(self):
            src, dst = self.refs
            for i in self.others:
                copy(src.at[i], dst.at[self.here], *self.sems, self.device(i)).start()
            self.own.start()

        def arrive(self):
            self.own.wait()
            self.all.wait_recv()

    a_one, a_two, b_one, b_two = [], [], [], []
    for h in range(2):
        a_sems = [(a_send.at[s], a_recv.at[s], own_sem.at[s]) for s in (h, 2 + h)]
        b_sems = [(b_send.at[s], b_recv.at[s], own_sem.at[4 + s]) for s in (h, 2 + h)]
        a_one.append(Exchange(a_spec.at[h], a_got.at[h], *a_sems[0], True))
        a_two.append(Exchange(a_turn.at[h], a_col.at[h], *a_sems[1], False))
        b_one.append(Exchange(b_spec.at[h], b_got.at[h], *b_sems[0], False))
        b_two.append(Exchange(b_turn.at[h], b_col.at[h], *b_sems[1], True))

    pl.semaphore_wait(barrier, n_y + n_c - 1)
    for h in range(2):
        a_one[h].start()
        b_one[h].start()

    for load in loads[2:]:
        load.wait()
    shape = (plane // LANES, LANES)
    place = lax.broadcasted_iota(jnp.int32, shape, 0) * LANES
    place = place + lax.broadcasted_iota(jnp.int32, shape, 1)
    antenna = place // channels
    device = place % channels
    of_a = device // n_y * 2 * n_y + device % n_y * 2 + k
    of_b = device % n_c * 2 * n_y + device // n_c * 2 + k
    row_id = jnp.where(antenna < 2, of_a, of_b) * 4 + antenna

    def look_up(index, row_of, dtype):
        group = index // LANES
        within = index % LANES
        found = jnp.zeros(shape, dtype)
        for h in range(antennas // LANES):
            row = jnp.broadcast_to(row_of(h), shape)
            got = jnp.take_along_axis(row, within, axis=1, mode="promise_in_bounds")
            found = jnp.where(group == h, got, found)
        return found

    def part_of(h):
        return slice(h * LANES, (h + 1) * LANES)

    ids = look_up(row_id, lambda h: wiring_ref[h : h + 1, :], jnp.int32)
    channel = c * n_y + y
    per_turn = 1.0 + channel.astype(F32) / channels
    norm = 1.0 / math.sqrt(antennas)
    own_row = lax.broadcasted_iota(jnp.int32, (n_y, LANES), 0) == y

    def gain_row(part, h):
        rows = gains_ref[part, :, part_of(h)]
        return jnp.sum(jnp.where(own_row, rows, 0.0), axis=0, keepdims=True)

    tab_ref[0] = look_up(ids, lambda h: pos_ref[0:1, part_of(h)], F32) * per_turn
    tab_ref[1] = look_up(ids, lambda h: pos_ref[1:2, part_of(h)], F32) * per_turn
    g_re = look_up(ids, lambda h: gain_row(0, h), F32) * norm
    g_im = look_up(ids, lambda h: gain_row(1, h), F32) * norm
    tab_ref[2] = g_re
    tab_ref[3] = g_im
    tab_ref[4] = 2.0 * g_re
    tab_ref[5] = 2.0 * g_im
    for i in range(2):
        dirs_ref[i] = jnp.broadcast_to(dir_ref[i : i + 1, :], (LANES, beams)).T

    sine, cosine = half_angle_coefficients()
    blocks = beams // ROWS

    def weights_block(i, carry):
        r = i // blocks
        first = pl.multiple_of(lax.rem(i, blocks) * ROWS, ROWS)
        columns = pl.ds(pl.multiple_of(r * LANES, LANES), LANES)
        px, py, gr, gi, gr2, gi2 = [tab_ref[n, pl.ds(r, 1), :] for n in range(6)]
        turns = dirs_ref[0, pl.ds(first, ROWS), :] * px + dirs_ref[1, pl.ds(first, ROWS), :] * py
        turn = turns - jnp.round(turns)
        square = turn * turn
        s = sine[-1]
        for coefficient in sine[-2::-1]:
            s = s * square + coefficient
        s = s * turn
        q = cosine[-1]
        for coefficient in cosine[-2::-1]:
            q = q * square + coefficient
        wre_ref[pl.ds(first, ROWS), columns] = (gr + s * (gi2 * q - gr2 * s)).astype(BF16)
        wim_ref[pl.ds(first, ROWS), columns] = (gi - s * (gi2 * s + gr2 * q)).astype(BF16)
        return carry

    steps = plane // LANES * blocks
    lax.fori_loop(0, steps // 2, weights_block, 0)
    for h in range(2):
        a_one[h].arrive()
        a_turn[h] = jnp.swapaxes(a_got[h], 0, 1)
        a_two[h].start()
        b_one[h].arrive()
        b_turn[h] = jnp.swapaxes(b_got[h], 0, 1)
        b_two[h].start()
    lax.fori_loop(steps // 2, steps, weights_block, 0)

    values = delays_ref[...].astype(F32).astype(BF16)
    source = lax.broadcasted_iota(jnp.int32, (channels, channels), 0)
    position = lax.broadcasted_iota(jnp.int32, (channels, channels), 1)
    tiles = channels // 4
    piece = position % tiles * 4 + position // tiles
    moved = (source == piece % n_c * n_y + piece // n_c).astype(F32).astype(BF16)
    dm_ref[...] = dot(values, moved, TN)
    mine = dm_ref[pl.ds(pl.multiple_of(board % 4 * TB, TB), TB), :]
    for d in range(TB):
        hot_ref[d * TB : (d + 1) * TB, :] = (mine == float(d)).astype(F32).astype(BF16)

    for h in range(2):
        a_two[h].arrive()
        b_two[h].arrive()

    rows = (2 * channels, 2 * SPECTRA)
    columns = jnp.concatenate([a_col[...].reshape(rows), b_col[...].reshape(rows)], axis=0)

    def beams_of(which):
        rows = pl.ds(pl.multiple_of(which * half_beams, half_beams), half_beams)
        with_re = dot(wre_ref[rows, :], columns, NN)
        with_im = dot(wim_ref[rows, :], columns, NN)
        return (
            with_re[:, :SPECTRA] - with_im[:, SPECTRA:],
            with_re[:, SPECTRA:] + with_im[:, :SPECTRA],
        )

    give_re, give_im = beams_of(1 - k)
    give_ref[0] = give_re
    give_ref[1] = give_im
    swap = copy(give_ref, take_ref, x_send, x_recv, partner)
    swap.start()
    keep_re, keep_im = beams_of(k)
    swap.wait_recv()
    beam_re = keep_re + take_ref[0]
    beam_im = keep_im + take_ref[1]
    energy = beam_re * beam_re + beam_im * beam_im

    high = energy.astype(BF16)
    low = (energy - high.astype(F32)).astype(BF16)
    from_s = lax.broadcasted_iota(jnp.int32, (SPECTRA, LANES), 0)
    to_t = lax.broadcasted_iota(jnp.int32, (SPECTRA, LANES), 1)
    mean = jnp.where(from_s // AVG == to_t % TB, 1.0 / AVG, 0.0).astype(BF16)
    power = dot(high, mean, NN) + dot(low, mean, NN)
    beam = lax.broadcasted_iota(jnp.int32, (half_beams, LANES), 0)
    slot = lax.broadcasted_iota(jnp.int32, (half_beams, LANES), 1)
    power = jnp.where(beam % 4 == slot // TB, power, 0.0).astype(BF16)
    to_row = lax.broadcasted_iota(jnp.int32, (half_beams // 4, half_beams), 0)
    of_beam = lax.broadcasted_iota(jnp.int32, (half_beams // 4, half_beams), 1)
    gather = (of_beam // 4 == to_row).astype(F32).astype(BF16)
    piece_ref[...] = dot(gather, power, NN).reshape(half_c, 4, LANES).astype(BF16)

    holds = c // half_c == k
    count = half_c * n_y

    def p_copy(index, to_y):
        return copy(
            piece_ref.at[index],
            pow_ref.at[mine_at],
            p_send,
            p_recv.at[y],
            (k * half_c + index, 2 * to_y + k),
        )

    indices = [h * n_x + (x + dx) % n_x for dx in far_first(n_x) for h in range(half_c // n_x)]
    for to_y in places:
        for index in indices:
            p_copy(index, to_y).start()
    for index in indices:

        @pl.when(k * half_c + index != c)
        def _():
            p_copy(index, y).start()

    def group(source, size):
        return pow_ref.at[pl.ds(pl.multiple_of(source * n_c, n_c), size)]

    def forward(source):
        rows = group(source, n_c)
        return copy(rows, rows, f_send.at[source], p_recv.at[source], partner)

    def group_wait(source, size):
        rows = group(source, size)
        copy(rows, rows, p_send, p_recv.at[source], partner).wait_recv()

    @pl.when(holds)
    def _():
        own_p = pltpu.make_async_copy(
            piece_ref.at[lax.rem(c, half_c)], pow_ref.at[mine_at], own_sem.at[8]
        )
        own_p.start()
        own_p.wait()
        group_wait(y, n_c - 1)
        forward(y).start()

        def g_wait(i, carry):
            source = lax.rem(y + i, n_y)
            group_wait(source, n_c)
            forward(source).start()
            return carry

        lax.fori_loop(1, n_y, g_wait, 0)

    @pl.when(jnp.logical_not(holds))
    def _():
        def f_wait(i, carry):
            forward(i).wait_recv()
            return carry

        lax.fori_loop(0, n_y, f_wait, 0)

    series = jnp.swapaxes(pow_ref[...].reshape(tiles, 16, LANES), 0, 1)

    def put(first):
        rows = pl.ds(first, 4)
        return pltpu.make_async_copy(made_ref.at[rows], out_hbm.at[rows], out_sem.at[first // 4])

    for pair in range(2):
        both = [
            jnp.concatenate([series[4 * r + 2 * pair + j] for r in range(4)], axis=0)
            for j in range(2)
        ]
        sums = dot(hot_ref[...], jnp.concatenate(both, axis=1), NN)
        for j in range(2):
            total = sums[:, j * LANES : (j + 1) * LANES]
            step = TB // 2
            while step:
                rows = step * TB
                total = total[:rows] + rotate(total[rows:], step)
                step //= 2
            mean_of = total
            step = TB // 2
            while step:
                mean_of = mean_of + rotate(mean_of, step)
                step //= 2
            result = (total - mean_of * (1.0 / TB)) * (1.0 / math.sqrt(channels))
            first = 4 * (2 * pair + j)
            for q in range(4):
                made_ref[first + q] = result[:, q * TB : (q + 1) * TB]
            put(first).start()

    for one in a_one + a_two + b_one + b_two:
        one.all.wait_send()
    swap.wait_send()

    @pl.when(holds)
    def _():
        rows = pow_ref.at[pl.ds(0, count - 1)]
        copy(rows, rows, p_send, p_recv.at[0], partner).wait_send()

        def f_sent(i, carry):
            forward(i).wait_send()
            return carry

        lax.fori_loop(0, n_y, f_sent, 0)

    @pl.when(jnp.logical_not(holds))
    def _():
        rows = pow_ref.at[pl.ds(0, count)]
        copy(rows, rows, p_send, p_recv.at[0], partner).wait_send()

    for first in range(0, 16, 4):
        put(first).wait()


def shards(n_c, n_y, voltages, wiring, positions, directions, gains, delays):
    channels = n_c * n_y
    frame = 2 * channels
    plane = 4 * channels
    beams = 16 * n_c
    half_beams = beams // 2
    samples = voltages.reshape(LOCAL_ANTENNAS, SPECTRA * frame // LANES, LANES).transpose(1, 0, 2)
    samples = samples.reshape(SPECTRA, frame // LANES * LOCAL_ANTENNAS, LANES)
    table = filter_rows(channels, n_c, n_y)
    ids = wiring.reshape(-1, LANES)
    operands = (samples, table, ids, positions, directions, gains, delays)
    loaded = [pltpu.VMEM(x.shape, x.dtype) for x in operands[:-1]]
    loaded.append(pltpu.VMEM((channels, LANES), delays.dtype))
    dma = pltpu.SemaphoreType.DMA
    by_y = pltpu.VMEM((2, n_y, n_c, 2 * SPECTRA), BF16)
    by_c = pltpu.VMEM((2, n_c, n_y, 2 * SPECTRA), BF16)
    return pl.pallas_call(
        functools.partial(kernel, n_c, n_y),
        out_shape=jax.ShapeDtypeStruct((16, TB, TB), F32),
        in_specs=[pl.BlockSpec(memory_space=pl.ANY)] * len(operands),
        out_specs=pl.BlockSpec(memory_space=pl.ANY),
        scratch_shapes=[
            *loaded,
            *[by_y, by_y, by_c, by_c],
            *[by_c, by_c, by_y, by_y],
            pltpu.VMEM((6, plane // LANES, LANES), F32),
            pltpu.VMEM((2, beams, LANES), F32),
            pltpu.VMEM((beams, plane), BF16),
            pltpu.VMEM((beams, plane), BF16),
            pltpu.VMEM((2, half_beams, SPECTRA), F32),
            pltpu.VMEM((2, half_beams, SPECTRA), F32),
            pltpu.VMEM((n_c // 2, 4, LANES), BF16),
            pltpu.VMEM((channels, 4, LANES), BF16),
            pltpu.VMEM((LANES, channels), F32),
            pltpu.VMEM((TB * TB, channels), BF16),
            pltpu.VMEM((16, TB, TB), F32),
            dma((len(operands),)),
            *[dma((4,))] * 4,
            dma,
            dma,
            dma,
            dma((n_y,)),
            dma((n_y,)),
            dma((9,)),
            dma((4,)),
        ],
        compiler_params=pltpu.CompilerParams(
            collective_id=0, has_side_effects=True, vmem_limit_bytes=60 * 1024 * 1024
        ),
    )(*operands)


def solution(mesh):
    n_c = mesh.shape["crate"]
    n_y = mesh.shape["board"] // 2
    in_specs = (P(("crate", "board"), None), P(), P(), P(), P(None, "crate", None), P())
    return jax.shard_map(
        functools.partial(shards, n_c, n_y),
        mesh=mesh,
        in_specs=in_specs,
        out_specs=P("crate", "board", None),
        check_vma=False,
    )
```

```python
import functools
import math

import jax
import jax.numpy as jnp
import numpy as np
from jax import lax
from jax.experimental import pallas as pl
from jax.experimental.pallas import tpu as pltpu
from jax.sharding import PartitionSpec as P

AVG = 4
TB = 32
LOCAL_ANTENNAS = 4
SPECTRA = 128
LANES = 128
ROWS = 64
MESH = pl.DeviceIdType.MESH
F32 = jnp.float32
BF16 = jnp.bfloat16

NT = (((1,), (1,)), ((), ()))
TN = (((0,), (0,)), ((), ()))
NN = (((1,), (0,)), ((), ()))


def half_angle_coefficients():
    nodes = np.cos((np.arange(400) + 0.5) * np.pi / 400) * 0.125 + 0.125
    root = np.sqrt(nodes)
    sine = np.polynomial.chebyshev.Chebyshev.fit(
        nodes, np.sin(np.pi * root) / root, 4, domain=[0, 0.25]
    ).convert(kind=np.polynomial.Polynomial)
    cosine = np.polynomial.chebyshev.Chebyshev.fit(
        nodes, np.cos(np.pi * root), 5, domain=[0, 0.25]
    ).convert(kind=np.polynomial.Polynomial)
    return [float(x) for x in sine.coef], [float(x) for x in cosine.coef]


def filter_rows(channels, n_c, n_y):
    frame = 2 * channels
    sample = np.arange(frame)
    window = 0.5 - 0.5 * np.cos(2 * np.pi / frame * sample)
    channel = (np.arange(n_c)[None, :] * n_y + np.arange(n_y)[:, None]).reshape(-1)
    angle = 2 * np.pi / frame * (channel[:, None] * sample[None, :] % frame)
    scale = 1.0 / math.sqrt(3.0 * frame / 8.0)
    table = np.concatenate([np.cos(angle), -np.sin(angle)], axis=0) * window[None, :] * scale
    return jnp.asarray(table.astype(np.float32)).astype(BF16)


def far_first(size):
    return sorted(range(size), key=lambda d: -min(d, size - d))


def dot(a, b, dims):
    return lax.dot_general(a, b, dims, preferred_element_type=F32)


def rotate(x, k):
    lane = lax.broadcasted_iota(jnp.int32, x.shape, x.ndim - 1)
    return jnp.take_along_axis(
        x, lane // TB * TB + (lane + k) % TB, axis=x.ndim - 1, mode="promise_in_bounds"
    )


def kernel(
    n_c,
    n_y,
    volt_hbm,
    filt_hbm,
    wiring_hbm,
    pos_hbm,
    dir_hbm,
    gains_hbm,
    delays_hbm,
    made_ref,
    volt_ref,
    filt_ref,
    wiring_ref,
    pos_ref,
    dir_ref,
    gains_ref,
    delays_ref,
    a_spec,
    a_got,
    a_turn,
    a_col,
    b_spec,
    b_got,
    b_turn,
    b_col,
    tab_ref,
    dirs_ref,
    wre_ref,
    wim_ref,
    give_ref,
    take_ref,
    piece_ref,
    pow_ref,
    dm_ref,
    hot_ref,
    in_sem,
    a_send,
    a_recv,
    b_send,
    b_recv,
    x_send,
    x_recv,
    p_send,
    p_recv,
    f_send,
    own_sem,
):
    c = lax.axis_index("crate")
    board = lax.axis_index("board")
    y = board // 2
    k = board % 2
    channels = n_c * n_y
    antennas = 8 * channels
    plane = 4 * channels
    beams = 16 * n_c
    half_beams = beams // 2
    half_c = n_c // 2
    partner = (c, 2 * y + 1 - k)
    n_x = min(8, n_c)
    n_z = n_c // n_x
    x = c % n_x
    z = c // n_x
    mine_at = y * n_c + c

    steps_c = [(dz, dx) for dz in range(n_z) for dx in range(n_x)]
    steps_c.sort(key=lambda s: -min(s[0], n_z - s[0]) - min(s[1], n_x - s[1]))
    crates = [(z + dz) % n_z * n_x + (x + dx) % n_x for dz, dx in steps_c[:-1]]
    places = [(y + dy) % n_y for dy in far_first(n_y)[:-1]]

    offset = pl.multiple_of(board // 4 * LANES, LANES)
    pairs = [
        (volt_hbm, volt_ref),
        (filt_hbm, filt_ref),
        (wiring_hbm, wiring_ref),
        (pos_hbm, pos_ref),
        (dir_hbm, dir_ref),
        (gains_hbm, gains_ref),
        (delays_hbm.at[:, pl.ds(offset, LANES)], delays_ref),
    ]
    loads = [pltpu.make_async_copy(*pair, in_sem.at[i]) for i, pair in enumerate(pairs)]
    for load in loads:
        load.start()

    barrier = pltpu.get_barrier_semaphore()
    for device in [(i, board) for i in crates] + [(c, 2 * i + k) for i in places] + [partner]:
        pl.semaphore_signal(barrier, inc=1, device_id=device, device_id_type=MESH)

    loads[0].wait()
    loads[1].wait()
    turned = jnp.swapaxes(volt_ref[...], 0, 1)
    frame_rows = turned.shape[0] // LOCAL_ANTENNAS

    def spectra(antenna):
        samples = jnp.concatenate(
            [turned[LOCAL_ANTENNAS * q + antenna] for q in range(frame_rows)], axis=1
        )
        rows = dot(filt_ref[...], samples, NT).reshape(2, n_y, n_c, SPECTRA)
        for part in range(2):
            lanes = slice(part * SPECTRA, (part + 1) * SPECTRA)
            if antenna < 2:
                a_spec[antenna, :, :, lanes] = rows[part].astype(BF16)
            else:
                b_spec[antenna - 2, :, :, lanes] = jnp.swapaxes(rows[part], 0, 1).astype(BF16)

    spectra(0)
    spectra(2)

    def copy(src, dst, send, recv, device):
        return pltpu.make_async_remote_copy(
            src_ref=src,
            dst_ref=dst,
            send_sem=send,
            recv_sem=recv,
            device_id=device,
            device_id_type=MESH,
        )

    class Exchange:
        def __init__(self, src, dst, send, recv, own_sem, along_y):
            self.refs = (src, dst)
            self.sems = (send, recv)
            self.here, self.others = (y, places) if along_y else (c, crates)
            self.device = (lambda i: (c, 2 * i + k)) if along_y else (lambda i: (i, board))
            own = (src.at[self.here], dst.at[self.here], own_sem)
            self.own = pltpu.make_async_copy(*own)
            count = pl.ds(0, len(self.others))
            self.all = copy(src.at[count], dst.at[count], send, recv, partner)

        def start(self):
            src, dst = self.refs
            for i in self.others:
                copy(src.at[i], dst.at[self.here], *self.sems, self.device(i)).start()
            self.own.start()

        def arrive(self):
            self.own.wait()
            self.all.wait_recv()

    a_one, a_two, b_one, b_two = [], [], [], []
    for h in range(2):
        a_sems = [(a_send.at[s], a_recv.at[s], own_sem.at[s]) for s in (h, 2 + h)]
        b_sems = [(b_send.at[s], b_recv.at[s], own_sem.at[4 + s]) for s in (h, 2 + h)]
        a_one.append(Exchange(a_spec.at[h], a_got.at[h], *a_sems[0], True))
        a_two.append(Exchange(a_turn.at[h], a_col.at[h], *a_sems[1], False))
        b_one.append(Exchange(b_spec.at[h], b_got.at[h], *b_sems[0], False))
        b_two.append(Exchange(b_turn.at[h], b_col.at[h], *b_sems[1], True))

    pl.semaphore_wait(barrier, n_y + n_c - 1)
    a_one[0].start()
    b_one[0].start()
    spectra(1)
    spectra(3)
    a_one[1].start()
    b_one[1].start()

    for load in loads[2:]:
        load.wait()
    shape = (plane // LANES, LANES)
    place = lax.broadcasted_iota(jnp.int32, shape, 0) * LANES
    place = place + lax.broadcasted_iota(jnp.int32, shape, 1)
    antenna = place // channels
    device = place % channels
    of_a = device // n_y * 2 * n_y + device % n_y * 2 + k
    of_b = device % n_c * 2 * n_y + device // n_c * 2 + k
    row_id = jnp.where(antenna < 2, of_a, of_b) * 4 + antenna

    def look_up(index, row_of, dtype):
        group = index // LANES
        within = index % LANES
        found = jnp.zeros(shape, dtype)
        for h in range(antennas // LANES):
            row = jnp.broadcast_to(row_of(h), shape)
            got = jnp.take_along_axis(row, within, axis=1, mode="promise_in_bounds")
            found = jnp.where(group == h, got, found)
        return found

    def part_of(h):
        return slice(h * LANES, (h + 1) * LANES)

    ids = look_up(row_id, lambda h: wiring_ref[h : h + 1, :], jnp.int32)
    channel = c * n_y + y
    per_turn = 1.0 + channel.astype(F32) / channels
    norm = 1.0 / math.sqrt(antennas)
    own_row = lax.broadcasted_iota(jnp.int32, (n_y, LANES), 0) == y

    def gain_row(part, h):
        rows = gains_ref[part, :, part_of(h)]
        return jnp.sum(jnp.where(own_row, rows, 0.0), axis=0, keepdims=True)

    tab_ref[0] = look_up(ids, lambda h: pos_ref[0:1, part_of(h)], F32) * per_turn
    tab_ref[1] = look_up(ids, lambda h: pos_ref[1:2, part_of(h)], F32) * per_turn
    g_re = look_up(ids, lambda h: gain_row(0, h), F32) * norm
    g_im = look_up(ids, lambda h: gain_row(1, h), F32) * norm
    tab_ref[2] = g_re
    tab_ref[3] = g_im
    tab_ref[4] = 2.0 * g_re
    tab_ref[5] = 2.0 * g_im
    for i in range(2):
        dirs_ref[i] = jnp.broadcast_to(dir_ref[i : i + 1, :], (LANES, beams)).T

    sine, cosine = half_angle_coefficients()
    blocks = beams // ROWS

    def weights_block(i, carry):
        r = i // blocks
        first = pl.multiple_of(lax.rem(i, blocks) * ROWS, ROWS)
        columns = pl.ds(pl.multiple_of(r * LANES, LANES), LANES)
        px, py, gr, gi, gr2, gi2 = [tab_ref[n, pl.ds(r, 1), :] for n in range(6)]
        turns = dirs_ref[0, pl.ds(first, ROWS), :] * px + dirs_ref[1, pl.ds(first, ROWS), :] * py
        turn = turns - jnp.round(turns)
        square = turn * turn
        s = sine[-1]
        for coefficient in sine[-2::-1]:
            s = s * square + coefficient
        s = s * turn
        q = cosine[-1]
        for coefficient in cosine[-2::-1]:
            q = q * square + coefficient
        wre_ref[pl.ds(first, ROWS), columns] = (gr + s * (gi2 * q - gr2 * s)).astype(BF16)
        wim_ref[pl.ds(first, ROWS), columns] = (gi - s * (gi2 * s + gr2 * q)).astype(BF16)
        return carry

    steps = plane // LANES * blocks
    lax.fori_loop(0, steps // 2, weights_block, 0)
    for h in range(2):
        a_one[h].arrive()
        a_turn[h] = jnp.swapaxes(a_got[h], 0, 1)
        a_two[h].start()
        b_one[h].arrive()
        b_turn[h] = jnp.swapaxes(b_got[h], 0, 1)
        b_two[h].start()
    lax.fori_loop(steps // 2, steps, weights_block, 0)

    values = delays_ref[...].astype(F32).astype(BF16)
    source = lax.broadcasted_iota(jnp.int32, (channels, channels), 0)
    position = lax.broadcasted_iota(jnp.int32, (channels, channels), 1)
    tiles = channels // 4
    piece = position % tiles * 4 + position // tiles
    moved = (source == piece % n_c * n_y + piece // n_c).astype(F32).astype(BF16)
    dm_ref[...] = dot(values, moved, TN)
    mine = dm_ref[pl.ds(pl.multiple_of(board % 4 * TB, TB), TB), :]
    for d in range(TB):
        rows = slice(d % 8 * TB, (d % 8 + 1) * TB)
        hot_ref[rows, d // 8 * channels : (d // 8 + 1) * channels] = (
            (mine == float(d)).astype(F32).astype(BF16)
        )

    for h in range(2):
        a_two[h].arrive()
        b_two[h].arrive()

    rows = (2 * channels, 2 * SPECTRA)
    columns = jnp.concatenate([a_col[...].reshape(rows), b_col[...].reshape(rows)], axis=0)

    chunks = half_c // n_x
    size = half_beams // chunks

    def beams_of(which, h):
        rows = pl.ds(pl.multiple_of(which * half_beams + h * size, size), size)
        with_re = dot(wre_ref[rows, :], columns, NN)
        with_im = dot(wim_ref[rows, :], columns, NN)
        return (
            with_re[:, :SPECTRA] - with_im[:, SPECTRA:],
            with_re[:, SPECTRA:] + with_im[:, :SPECTRA],
        )

    swaps = []
    for h in range(chunks):
        give_ref[h, 0], give_ref[h, 1] = beams_of(1 - k, h)
        swaps.append(copy(give_ref.at[h], take_ref.at[h], x_send.at[h], x_recv.at[h], partner))
        swaps[h].start()

    from_s = lax.broadcasted_iota(jnp.int32, (SPECTRA, LANES), 0)
    to_t = lax.broadcasted_iota(jnp.int32, (SPECTRA, LANES), 1)
    mean = jnp.where(from_s // AVG == to_t % TB, 1.0 / AVG, 0.0).astype(BF16)
    beam = lax.broadcasted_iota(jnp.int32, (size, LANES), 0)
    slot = lax.broadcasted_iota(jnp.int32, (size, LANES), 1)
    to_row = lax.broadcasted_iota(jnp.int32, (size // 4, size), 0)
    of_beam = lax.broadcasted_iota(jnp.int32, (size // 4, size), 1)
    gather = (of_beam // 4 == to_row).astype(F32).astype(BF16)

    def powers(h):
        keep_re, keep_im = beams_of(k, h)
        swaps[h].wait_recv()
        beam_re = keep_re + take_ref[h, 0]
        beam_im = keep_im + take_ref[h, 1]
        energy = beam_re * beam_re + beam_im * beam_im
        high = energy.astype(BF16)
        low = (energy - high.astype(F32)).astype(BF16)
        power = dot(high, mean, NN) + dot(low, mean, NN)
        power = jnp.where(beam % 4 == slot // TB, power, 0.0).astype(BF16)
        rows = dot(gather, power, NN).reshape(n_x, 4, LANES)
        piece_ref[h * n_x : (h + 1) * n_x] = rows.astype(BF16)

    holds = c // half_c == k
    count = half_c * n_y

    def p_copy(index, to_y):
        return copy(
            piece_ref.at[index],
            pow_ref.at[mine_at],
            p_send,
            p_recv.at[y],
            (k * half_c + index, 2 * to_y + k),
        )

    for h in range(chunks):
        powers(h)
        indices = [h * n_x + (x + dx) % n_x for dx in far_first(n_x)]
        for to_y in places:
            for index in indices:
                p_copy(index, to_y).start()
        for index in indices:

            @pl.when(k * half_c + index != c)
            def _():
                p_copy(index, y).start()

    def group(source, size):
        return pow_ref.at[pl.ds(pl.multiple_of(source * n_c, n_c), size)]

    def forward(source):
        rows = group(source, n_c)
        return copy(rows, rows, f_send.at[source], p_recv.at[source], partner)

    def group_wait(source, size):
        rows = group(source, size)
        copy(rows, rows, p_send, p_recv.at[source], partner).wait_recv()

    @pl.when(holds)
    def _():
        own_p = pltpu.make_async_copy(
            piece_ref.at[lax.rem(c, half_c)], pow_ref.at[mine_at], own_sem.at[8]
        )
        own_p.start()
        own_p.wait()
        group_wait(y, n_c - 1)
        forward(y).start()

        def g_wait(i, carry):
            source = lax.rem(y + i, n_y)
            group_wait(source, n_c)
            forward(source).start()
            return carry

        lax.fori_loop(1, n_y, g_wait, 0)

    @pl.when(jnp.logical_not(holds))
    def _():
        def f_wait(i, carry):
            forward(i).wait_recv()
            return carry

        lax.fori_loop(0, n_y, f_wait, 0)

    series = jnp.swapaxes(pow_ref[...].reshape(tiles, 16, LANES), 0, 1)
    flat = series.reshape(16 * tiles, LANES)
    source = lax.broadcasted_iota(jnp.int32, (LANES, LANES), 0)
    place = lax.broadcasted_iota(jnp.int32, (LANES, LANES), 1)

    def shift(n):
        chosen = source == place // TB * TB + (place + 8 * n) % TB
        return chosen.astype(F32).astype(BF16)

    near = dot(flat, jnp.concatenate([shift(1), shift(2)], axis=1), NN).astype(BF16)
    shifted = [flat, near[:, :LANES], near[:, LANES:], dot(flat, shift(3), NN).astype(BF16)]
    shifted = [v.reshape(16, tiles, LANES) for v in shifted]
    for pair in range(2):
        both = [
            jnp.concatenate([v[4 * r + 2 * pair + j] for v in shifted for r in range(4)], axis=0)
            for j in range(2)
        ]
        sums = dot(hot_ref[...], jnp.concatenate(both, axis=1), NN)
        mean_of = []
        for j in range(2):
            level = dot(jnp.ones((8, channels), BF16), both[j][:channels], NN)
            step = TB // 2
            while step:
                level = level + rotate(level, step)
                step //= 2
            mean_of.append(level[:1] * (1.0 / TB))
        for j in range(2):
            total = sums[:, j * LANES : (j + 1) * LANES]
            step = 4
            while step:
                rows = step * TB
                total = total[:rows] + rotate(total[rows:], step)
                step //= 2
            result = (total - mean_of[j]) * (1.0 / math.sqrt(channels))
            first = 4 * (2 * pair + j)
            for q in range(4):
                made_ref[first + q] = result[:, q * TB : (q + 1) * TB]

    for one in a_one + a_two + b_one + b_two:
        one.all.wait_send()
    for swap in swaps:
        swap.wait_send()

    @pl.when(holds)
    def _():
        rows = pow_ref.at[pl.ds(0, count - 1)]
        copy(rows, rows, p_send, p_recv.at[0], partner).wait_send()

        def f_sent(i, carry):
            forward(i).wait_send()
            return carry

        lax.fori_loop(0, n_y, f_sent, 0)

    @pl.when(jnp.logical_not(holds))
    def _():
        rows = pow_ref.at[pl.ds(0, count)]
        copy(rows, rows, p_send, p_recv.at[0], partner).wait_send()


def shards(n_c, n_y, voltages, wiring, positions, directions, gains, delays):
    channels = n_c * n_y
    frame = 2 * channels
    plane = 4 * channels
    beams = 16 * n_c
    half_beams = beams // 2
    chunks = n_c // 2 // min(8, n_c)
    samples = voltages.reshape(LOCAL_ANTENNAS, SPECTRA * frame // LANES, LANES).transpose(1, 0, 2)
    samples = samples.reshape(SPECTRA, frame // LANES * LOCAL_ANTENNAS, LANES)
    table = filter_rows(channels, n_c, n_y)
    ids = wiring.reshape(-1, LANES)
    operands = (samples, table, ids, positions, directions, gains, delays)
    loaded = [pltpu.VMEM(x.shape, x.dtype) for x in operands[:-1]]
    loaded.append(pltpu.VMEM((channels, LANES), delays.dtype))
    dma = pltpu.SemaphoreType.DMA
    by_y = pltpu.VMEM((2, n_y, n_c, 2 * SPECTRA), BF16)
    by_c = pltpu.VMEM((2, n_c, n_y, 2 * SPECTRA), BF16)
    return pl.pallas_call(
        functools.partial(kernel, n_c, n_y),
        out_shape=pltpu.VMEM((16, TB, TB), F32),
        in_specs=[pl.BlockSpec(memory_space=pl.ANY)] * len(operands),
        out_specs=pl.BlockSpec(memory_space=pltpu.VMEM),
        scratch_shapes=[
            *loaded,
            *[by_y, by_y, by_c, by_c],
            *[by_c, by_c, by_y, by_y],
            pltpu.VMEM((6, plane // LANES, LANES), F32),
            pltpu.VMEM((2, beams, LANES), F32),
            pltpu.VMEM((beams, plane), BF16),
            pltpu.VMEM((beams, plane), BF16),
            *[pltpu.VMEM((chunks, 2, half_beams // chunks, SPECTRA), F32)] * 2,
            pltpu.VMEM((n_c // 2, 4, LANES), BF16),
            pltpu.VMEM((channels, 4, LANES), BF16),
            pltpu.VMEM((LANES, channels), F32),
            pltpu.VMEM((8 * TB, 4 * channels), BF16),
            dma((len(operands),)),
            *[dma((4,))] * 4,
            *[dma((chunks,))] * 2,
            dma,
            dma((n_y,)),
            dma((n_y,)),
            dma((9,)),
        ],
        compiler_params=pltpu.CompilerParams(
            collective_id=0, has_side_effects=True, vmem_limit_bytes=60 * 1024 * 1024
        ),
    )(*operands)


def solution(mesh):
    n_c = mesh.shape["crate"]
    n_y = mesh.shape["board"] // 2
    in_specs = (P(("crate", "board"), None), P(), P(), P(), P(None, "crate", None), P())
    return jax.shard_map(
        functools.partial(shards, n_c, n_y),
        mesh=mesh,
        in_specs=in_specs,
        out_specs=P("crate", "board", None),
        check_vma=False,
    )
```

```python
import functools
import math

import jax
import jax.numpy as jnp
import numpy as np
from jax import lax
from jax.experimental import pallas as pl
from jax.experimental.pallas import tpu as pltpu
from jax.sharding import PartitionSpec as P

AVG = 4
TB = 32
LOCAL_ANTENNAS = 4
SPECTRA = 128
SIZE_X = 4
LANES = 128
ROWS = 64
MESH = pl.DeviceIdType.MESH
F32 = jnp.float32
BF16 = jnp.bfloat16

NT = (((1,), (1,)), ((), ()))
TN = (((0,), (0,)), ((), ()))
NN = (((1,), (0,)), ((), ()))


def half_angle_coefficients():
    nodes = np.cos((np.arange(400) + 0.5) * np.pi / 400) * 0.125 + 0.125
    root = np.sqrt(nodes)
    sine = np.polynomial.chebyshev.Chebyshev.fit(
        nodes, np.sin(np.pi * root) / root, 4, domain=[0, 0.25]
    ).convert(kind=np.polynomial.Polynomial)
    cosine = np.polynomial.chebyshev.Chebyshev.fit(
        nodes, np.cos(np.pi * root), 5, domain=[0, 0.25]
    ).convert(kind=np.polynomial.Polynomial)
    return [float(x) for x in sine.coef], [float(x) for x in cosine.coef]


def filter_rows(channels, n_c, n_y):
    frame = 2 * channels
    sample = np.arange(frame)
    window = 0.5 - 0.5 * np.cos(2 * np.pi / frame * sample)
    by_y = np.arange(n_c)[None, :] * n_y + np.arange(n_y)[:, None]
    by_z = by_y.reshape(n_y, -1, SIZE_X).transpose(1, 0, 2)
    scale = 1.0 / math.sqrt(3.0 * frame / 8.0)
    tables = []
    for channel in (by_y.reshape(-1), by_z.reshape(-1)):
        angle = 2 * np.pi / frame * (channel[:, None] * sample[None, :] % frame)
        table = np.concatenate([np.cos(angle), -np.sin(angle)], axis=0)
        tables.append(table * window[None, :] * scale)
    return jnp.asarray(np.stack(tables).astype(np.float32)).astype(BF16)


def far_first(size):
    return sorted(range(size), key=lambda d: -min(d, size - d))


def dot(a, b, dims):
    return lax.dot_general(a, b, dims, preferred_element_type=F32)


def rotate(x, k):
    lane = lax.broadcasted_iota(jnp.int32, x.shape, x.ndim - 1)
    return jnp.take_along_axis(
        x, lane // TB * TB + (lane + k) % TB, axis=x.ndim - 1, mode="promise_in_bounds"
    )


def kernel(
    n_c,
    n_y,
    volt_hbm,
    filt_hbm,
    wiring_hbm,
    pos_hbm,
    dir_hbm,
    gains_hbm,
    delays_hbm,
    made_ref,
    volt_ref,
    filt_ref,
    wiring_ref,
    pos_ref,
    dir_ref,
    gains_ref,
    delays_ref,
    a_spec,
    a_got,
    a_turn,
    a_col,
    b_spec,
    b_got,
    b_turn,
    b_col,
    tab_ref,
    dirs_ref,
    wre_ref,
    wim_ref,
    give_ref,
    take_ref,
    piece_ref,
    pow_ref,
    dm_ref,
    hot_ref,
    in_sem,
    a_send,
    a_recv,
    b_send,
    b_recv,
    x_send,
    x_recv,
    p_send,
    p_recv,
    f_send,
    own_sem,
):
    c = lax.axis_index("crate")
    board = lax.axis_index("board")
    y = board // 2
    k = board % 2
    channels = n_c * n_y
    antennas = 8 * channels
    plane = 4 * channels
    beams = 16 * n_c
    half_beams = beams // 2
    half_c = n_c // 2
    partner = (c, 2 * y + 1 - k)
    n_x = SIZE_X
    n_z = n_c // n_x
    x = c % n_x
    z = c // n_x
    mine_at = y * n_c + c

    steps_c = [(dz, dx) for dz in range(n_z) for dx in range(n_x)]
    steps_c.sort(key=lambda s: -min(s[0], n_z - s[0]) - min(s[1], n_x - s[1]))
    crates = [(z + dz) % n_z * n_x + (x + dx) % n_x for dz, dx in steps_c[:-1]]
    places = [(y + dy) % n_y for dy in far_first(n_y)[:-1]]
    places_z = [(z + dz) % n_z for dz in far_first(n_z)[:-1]]
    places_x = [(x + dx) % n_x for dx in far_first(n_x)[:-1]]
    steps_yx = [(dy, dx) for dy in range(n_y) for dx in range(n_x)]
    steps_yx.sort(key=lambda s: -min(s[0], n_y - s[0]) - min(s[1], n_x - s[1]))
    places_yx = [(y + dy) % n_y * n_x + (x + dx) % n_x for dy, dx in steps_yx[:-1]]

    offset = pl.multiple_of(board // 4 * LANES, LANES)
    pairs = [
        (volt_hbm, volt_ref),
        (filt_hbm, filt_ref),
        (wiring_hbm, wiring_ref),
        (pos_hbm, pos_ref),
        (dir_hbm, dir_ref),
        (gains_hbm, gains_ref),
        (delays_hbm.at[:, pl.ds(offset, LANES)], delays_ref),
    ]
    loads = [pltpu.make_async_copy(*pair, in_sem.at[i]) for i, pair in enumerate(pairs)]
    for load in loads:
        load.start()

    barrier = pltpu.get_barrier_semaphore()
    near_ones = [(c, 2 * i + k) for i in places] + [(z * n_x + i, board) for i in places_x]
    near_ones += [(i * n_x + x, board) for i in places_z] + [partner]
    for device in near_ones:
        pl.semaphore_signal(barrier, inc=1, device_id=device, device_id_type=MESH)

    loads[0].wait()
    loads[1].wait()
    turned = jnp.swapaxes(volt_ref[...], 0, 1)
    frame_rows = turned.shape[0] // LOCAL_ANTENNAS

    def spectra(antenna):
        samples = jnp.concatenate(
            [turned[LOCAL_ANTENNAS * q + antenna] for q in range(frame_rows)], axis=1
        )
        rows = dot(filt_ref[antenna // 2], samples, NT)
        first, spec_ref = ((n_y, a_spec), (n_z, b_spec))[antenna // 2]
        rows = rows.reshape(2, first, channels // first, SPECTRA).astype(BF16)
        for part in range(2):
            spec_ref[antenna % 2, :, :, part * SPECTRA : (part + 1) * SPECTRA] = rows[part]

    spectra(0)
    spectra(2)

    def copy(src, dst, send, recv, device):
        return pltpu.make_async_remote_copy(
            src_ref=src,
            dst_ref=dst,
            send_sem=send,
            recv_sem=recv,
            device_id=device,
            device_id_type=MESH,
        )

    class Exchange:
        def __init__(self, src, dst, send, recv, own_sem, along):
            self.refs = (src, dst)
            self.sems = (send, recv)
            self.here, self.others, self.device = along
            own = (src.at[self.here], dst.at[self.here], own_sem)
            self.own = pltpu.make_async_copy(*own)
            count = pl.ds(0, len(self.others))
            self.all = copy(src.at[count], dst.at[count], send, recv, partner)

        def start(self):
            src, dst = self.refs
            for i in self.others:
                copy(src.at[i], dst.at[self.here], *self.sems, self.device(i)).start()
            self.own.start()

        def arrive(self):
            self.own.wait()
            self.all.wait_recv()

    along_y = (y, places, lambda i: (c, 2 * i + k))
    over_c = (c, crates, lambda i: (i, board))
    along_z = (z, places_z, lambda i: (i * n_x + x, board))
    over_yx = (y * n_x + x, places_yx, lambda i: (z * n_x + i % n_x, i // n_x * 2 + k))
    a_one, a_two, b_one, b_two = [], [], [], []
    for h in range(2):
        a_sems = [(a_send.at[s], a_recv.at[s], own_sem.at[s]) for s in (h, 2 + h)]
        b_sems = [(b_send.at[s], b_recv.at[s], own_sem.at[4 + s]) for s in (h, 2 + h)]
        a_one.append(Exchange(a_spec.at[h], a_got.at[h], *a_sems[0], along_y))
        a_two.append(Exchange(a_turn.at[h], a_col.at[h], *a_sems[1], over_c))
        b_one.append(Exchange(b_spec.at[h], b_got.at[h], *b_sems[0], along_z))
        b_two.append(Exchange(b_turn.at[h], b_col.at[h], *b_sems[1], over_yx))

    pl.semaphore_wait(barrier, len(near_ones))
    a_one[0].start()
    b_one[0].start()
    spectra(1)
    spectra(3)
    a_one[1].start()
    b_one[1].start()

    for load in loads[2:]:
        load.wait()
    shape = (plane // LANES, LANES)
    place = lax.broadcasted_iota(jnp.int32, shape, 0) * LANES
    place = place + lax.broadcasted_iota(jnp.int32, shape, 1)
    antenna = place // channels
    device = place % channels
    of_a = device // n_y * 2 * n_y + device % n_y * 2 + k
    crate = device % n_z * n_x + device % n_c // n_z
    of_b = crate * 2 * n_y + device // n_c * 2 + k
    row_id = jnp.where(antenna < 2, of_a, of_b) * 4 + antenna

    def look_up(index, row_of, dtype):
        group = index // LANES
        within = index % LANES
        found = jnp.zeros(shape, dtype)
        for h in range(antennas // LANES):
            row = jnp.broadcast_to(row_of(h), shape)
            got = jnp.take_along_axis(row, within, axis=1, mode="promise_in_bounds")
            found = jnp.where(group == h, got, found)
        return found

    def part_of(h):
        return slice(h * LANES, (h + 1) * LANES)

    ids = look_up(row_id, lambda h: wiring_ref[h : h + 1, :], jnp.int32)
    channel = c * n_y + y
    per_turn = 1.0 + channel.astype(F32) / channels
    norm = 1.0 / math.sqrt(antennas)
    own_row = lax.broadcasted_iota(jnp.int32, (n_y, LANES), 0) == y

    def gain_row(part, h):
        rows = gains_ref[part, :, part_of(h)]
        return jnp.sum(jnp.where(own_row, rows, 0.0), axis=0, keepdims=True)

    tab_ref[0] = look_up(ids, lambda h: pos_ref[0:1, part_of(h)], F32) * per_turn
    tab_ref[1] = look_up(ids, lambda h: pos_ref[1:2, part_of(h)], F32) * per_turn
    g_re = look_up(ids, lambda h: gain_row(0, h), F32) * norm
    g_im = look_up(ids, lambda h: gain_row(1, h), F32) * norm
    tab_ref[2] = g_re
    tab_ref[3] = g_im
    tab_ref[4] = 2.0 * g_re
    tab_ref[5] = 2.0 * g_im
    for i in range(2):
        dirs_ref[i] = jnp.broadcast_to(dir_ref[i : i + 1, :], (LANES, beams)).T

    sine, cosine = half_angle_coefficients()
    blocks = beams // ROWS

    def weights_block(i, carry):
        r = i // blocks
        first = pl.multiple_of(lax.rem(i, blocks) * ROWS, ROWS)
        columns = pl.ds(pl.multiple_of(r * LANES, LANES), LANES)
        px, py, gr, gi, gr2, gi2 = [tab_ref[n, pl.ds(r, 1), :] for n in range(6)]
        turns = dirs_ref[0, pl.ds(first, ROWS), :] * px + dirs_ref[1, pl.ds(first, ROWS), :] * py
        turn = turns - jnp.round(turns)
        square = turn * turn
        s = sine[-1]
        for coefficient in sine[-2::-1]:
            s = s * square + coefficient
        s = s * turn
        q = cosine[-1]
        for coefficient in cosine[-2::-1]:
            q = q * square + coefficient
        wre_ref[pl.ds(first, ROWS), columns] = (gr + s * (gi2 * q - gr2 * s)).astype(BF16)
        wim_ref[pl.ds(first, ROWS), columns] = (gi - s * (gi2 * s + gr2 * q)).astype(BF16)
        return carry

    steps = plane // LANES * blocks
    lax.fori_loop(0, steps // 2, weights_block, 0)
    for h in range(2):
        a_one[h].arrive()
        a_turn[h] = jnp.swapaxes(a_got[h], 0, 1)
        b_one[h].arrive()
        a_two[h].start()
        b_turn[h] = jnp.swapaxes(b_got[h], 0, 1)
        b_two[h].start()
    lax.fori_loop(steps // 2, steps, weights_block, 0)

    values = delays_ref[...].astype(F32).astype(BF16)
    source = lax.broadcasted_iota(jnp.int32, (channels, channels), 0)
    position = lax.broadcasted_iota(jnp.int32, (channels, channels), 1)
    tiles = channels // 4
    piece = position % tiles * 4 + position // tiles
    moved = (source == piece % n_c * n_y + piece // n_c).astype(F32).astype(BF16)
    dm_ref[...] = dot(values, moved, TN)
    mine = dm_ref[pl.ds(pl.multiple_of(board % 4 * TB, TB), TB), :]
    for d in range(TB):
        rows = slice(d % 8 * TB, (d % 8 + 1) * TB)
        hot_ref[rows, d // 8 * channels : (d // 8 + 1) * channels] = (
            (mine == float(d)).astype(F32).astype(BF16)
        )

    for h in range(2):
        a_two[h].arrive()
        b_two[h].arrive()

    rows = (2 * channels, 2 * SPECTRA)
    columns = jnp.concatenate([a_col[...].reshape(rows), b_col[...].reshape(rows)], axis=0)

    chunks = 2
    size = half_beams // chunks
    served = half_c // chunks

    def beams_of(which, h):
        rows = pl.ds(pl.multiple_of(which * half_beams + h * size, size), size)
        with_re = dot(wre_ref[rows, :], columns, NN)
        with_im = dot(wim_ref[rows, :], columns, NN)
        return (
            with_re[:, :SPECTRA] - with_im[:, SPECTRA:],
            with_re[:, SPECTRA:] + with_im[:, :SPECTRA],
        )

    swaps = []
    for h in range(chunks):
        give_ref[h, 0], give_ref[h, 1] = beams_of(1 - k, h)
        swaps.append(copy(give_ref.at[h], take_ref.at[h], x_send.at[h], x_recv.at[h], partner))
        swaps[h].start()

    from_s = lax.broadcasted_iota(jnp.int32, (SPECTRA, LANES), 0)
    to_t = lax.broadcasted_iota(jnp.int32, (SPECTRA, LANES), 1)
    mean = jnp.where(from_s // AVG == to_t % TB, 1.0 / AVG, 0.0).astype(BF16)
    beam = lax.broadcasted_iota(jnp.int32, (size, LANES), 0)
    slot = lax.broadcasted_iota(jnp.int32, (size, LANES), 1)
    to_row = lax.broadcasted_iota(jnp.int32, (size // 4, size), 0)
    of_beam = lax.broadcasted_iota(jnp.int32, (size // 4, size), 1)
    gather = (of_beam // 4 == to_row).astype(F32).astype(BF16)

    kept = [beams_of(k, h) for h in range(chunks)]

    def powers(h):
        keep_re, keep_im = kept[h]
        swaps[h].wait_recv()
        beam_re = keep_re + take_ref[h, 0]
        beam_im = keep_im + take_ref[h, 1]
        energy = beam_re * beam_re + beam_im * beam_im
        high = energy.astype(BF16)
        low = (energy - high.astype(F32)).astype(BF16)
        power = dot(high, mean, NN) + dot(low, mean, NN)
        power = jnp.where(beam % 4 == slot // TB, power, 0.0).astype(BF16)
        rows = dot(gather, power, NN).reshape(served, 4, LANES)
        piece_ref[h * served : (h + 1) * served] = rows.astype(BF16)

    holds = c // half_c == k
    count = half_c * n_y

    def p_copy(index, to_y):
        return copy(
            piece_ref.at[index],
            pow_ref.at[mine_at],
            p_send,
            p_recv.at[y],
            (k * half_c + index, 2 * to_y + k),
        )

    for h in range(chunks):
        powers(h)
        tails = [h * served + (x + dx) % n_x for dx in far_first(n_x)]
        indices = [i + tail for tail in tails for i in range(0, served, n_x)]
        for to_y in places:
            for index in indices:
                p_copy(index, to_y).start()
        for index in indices:

            @pl.when(k * half_c + index != c)
            def _():
                p_copy(index, y).start()

    def group(source, size):
        return pow_ref.at[pl.ds(pl.multiple_of(source * n_c, n_c), size)]

    def forward(source):
        rows = group(source, n_c)
        return copy(rows, rows, f_send.at[source], p_recv.at[source], partner)

    def group_wait(source, size):
        rows = group(source, size)
        copy(rows, rows, p_send, p_recv.at[source], partner).wait_recv()

    @pl.when(holds)
    def _():
        own_p = pltpu.make_async_copy(
            piece_ref.at[lax.rem(c, half_c)], pow_ref.at[mine_at], own_sem.at[8]
        )
        own_p.start()
        own_p.wait()
        group_wait(y, n_c - 1)
        forward(y).start()

        def g_wait(i, carry):
            source = lax.rem(y + i, n_y)
            group_wait(source, n_c)
            forward(source).start()
            return carry

        lax.fori_loop(1, n_y, g_wait, 0)

    @pl.when(jnp.logical_not(holds))
    def _():
        def f_wait(i, carry):
            forward(i).wait_recv()
            return carry

        lax.fori_loop(0, n_y, f_wait, 0)

    series = jnp.swapaxes(pow_ref[...].reshape(tiles, 16, LANES), 0, 1)
    flat = series.reshape(16 * tiles, LANES)
    source = lax.broadcasted_iota(jnp.int32, (LANES, LANES), 0)
    place = lax.broadcasted_iota(jnp.int32, (LANES, LANES), 1)

    def shift(n):
        chosen = source == place // TB * TB + (place + 8 * n) % TB
        return chosen.astype(F32).astype(BF16)

    near = dot(flat, jnp.concatenate([shift(1), shift(2)], axis=1), NN).astype(BF16)
    shifted = [flat, near[:, :LANES], near[:, LANES:], dot(flat, shift(3), NN).astype(BF16)]
    shifted = [v.reshape(16, tiles, LANES) for v in shifted]
    for pair in range(2):
        both = [
            jnp.concatenate([v[4 * r + 2 * pair + j] for v in shifted for r in range(4)], axis=0)
            for j in range(2)
        ]
        sums = dot(hot_ref[...], jnp.concatenate(both, axis=1), NN)
        mean_of = []
        for j in range(2):
            level = dot(jnp.ones((8, channels), BF16), both[j][:channels], NN)
            step = TB // 2
            while step:
                level = level + rotate(level, step)
                step //= 2
            mean_of.append(level[:1] * (1.0 / TB))
        for j in range(2):
            total = sums[:, j * LANES : (j + 1) * LANES]
            step = 4
            while step:
                rows = step * TB
                total = total[:rows] + rotate(total[rows:], step)
                step //= 2
            result = (total - mean_of[j]) * (1.0 / math.sqrt(channels))
            first = 4 * (2 * pair + j)
            for q in range(4):
                made_ref[first + q] = result[:, q * TB : (q + 1) * TB]

    for one in a_one + a_two + b_one + b_two:
        one.all.wait_send()
    for swap in swaps:
        swap.wait_send()

    @pl.when(holds)
    def _():
        rows = pow_ref.at[pl.ds(0, count - 1)]
        copy(rows, rows, p_send, p_recv.at[0], partner).wait_send()

        def f_sent(i, carry):
            forward(i).wait_send()
            return carry

        lax.fori_loop(0, n_y, f_sent, 0)

    @pl.when(jnp.logical_not(holds))
    def _():
        rows = pow_ref.at[pl.ds(0, count)]
        copy(rows, rows, p_send, p_recv.at[0], partner).wait_send()


def shards(n_c, n_y, voltages, wiring, positions, directions, gains, delays):
    channels = n_c * n_y
    frame = 2 * channels
    plane = 4 * channels
    beams = 16 * n_c
    half_beams = beams // 2
    samples = voltages.reshape(LOCAL_ANTENNAS, SPECTRA * frame // LANES, LANES).transpose(1, 0, 2)
    samples = samples.reshape(SPECTRA, frame // LANES * LOCAL_ANTENNAS, LANES)
    table = filter_rows(channels, n_c, n_y)
    ids = wiring.reshape(-1, LANES)
    operands = (samples, table, ids, positions, directions, gains, delays)
    loaded = [pltpu.VMEM(x.shape, x.dtype) for x in operands[:-1]]
    loaded.append(pltpu.VMEM((channels, LANES), delays.dtype))
    dma = pltpu.SemaphoreType.DMA
    by_y = pltpu.VMEM((2, n_y, n_c, 2 * SPECTRA), BF16)
    by_c = pltpu.VMEM((2, n_c, n_y, 2 * SPECTRA), BF16)
    n_z = n_c // SIZE_X
    chunks = 2
    by_z = pltpu.VMEM((2, n_z, channels // n_z, 2 * SPECTRA), BF16)
    by_yx = pltpu.VMEM((2, channels // n_z, n_z, 2 * SPECTRA), BF16)
    return pl.pallas_call(
        functools.partial(kernel, n_c, n_y),
        out_shape=pltpu.VMEM((16, TB, TB), F32),
        in_specs=[pl.BlockSpec(memory_space=pl.ANY)] * len(operands),
        out_specs=pl.BlockSpec(memory_space=pltpu.VMEM),
        scratch_shapes=[
            *loaded,
            *[by_y, by_y, by_c, by_c],
            *[by_z, by_z, by_yx, by_yx],
            pltpu.VMEM((6, plane // LANES, LANES), F32),
            pltpu.VMEM((2, beams, LANES), F32),
            pltpu.VMEM((beams, plane), BF16),
            pltpu.VMEM((beams, plane), BF16),
            *[pltpu.VMEM((chunks, 2, half_beams // chunks, SPECTRA), F32)] * 2,
            pltpu.VMEM((n_c // 2, 4, LANES), BF16),
            pltpu.VMEM((channels, 4, LANES), BF16),
            pltpu.VMEM((LANES, channels), F32),
            pltpu.VMEM((8 * TB, 4 * channels), BF16),
            dma((len(operands),)),
            *[dma((4,))] * 4,
            *[dma((chunks,))] * 2,
            dma,
            dma((n_y,)),
            dma((n_y,)),
            dma((9,)),
        ],
        compiler_params=pltpu.CompilerParams(
            collective_id=0, has_side_effects=True, vmem_limit_bytes=60 * 1024 * 1024
        ),
    )(*operands)


def solution(mesh):
    n_c = mesh.shape["crate"]
    n_y = mesh.shape["board"] // 2
    in_specs = (P(("crate", "board"), None), P(), P(), P(), P(None, "crate", None), P())
    return jax.shard_map(
        functools.partial(shards, n_c, n_y),
        mesh=mesh,
        in_specs=in_specs,
        out_specs=P("crate", "board", None),
        check_vma=False,
    )
```

```python
import functools
import math

import jax
import jax.numpy as jnp
import numpy as np
from jax import lax
from jax.experimental import pallas as pl
from jax.experimental.pallas import tpu as pltpu
from jax.sharding import PartitionSpec as P

AVG = 4
TB = 32
LOCAL_ANTENNAS = 4
SPECTRA = 128
SIZE_X = 4
LANES = 128
ROWS = 64
MESH = pl.DeviceIdType.MESH
F32 = jnp.float32
BF16 = jnp.bfloat16

NT = (((1,), (1,)), ((), ()))
TN = (((0,), (0,)), ((), ()))
NN = (((1,), (0,)), ((), ()))


def half_angle_coefficients():
    nodes = np.cos((np.arange(400) + 0.5) * np.pi / 400) * 0.125 + 0.125
    root = np.sqrt(nodes)
    sine = np.polynomial.chebyshev.Chebyshev.fit(
        nodes, np.sin(np.pi * root) / root, 4, domain=[0, 0.25]
    ).convert(kind=np.polynomial.Polynomial)
    cosine = np.polynomial.chebyshev.Chebyshev.fit(
        nodes, np.cos(np.pi * root), 5, domain=[0, 0.25]
    ).convert(kind=np.polynomial.Polynomial)
    return [float(x) for x in sine.coef], [float(x) for x in cosine.coef]


def filter_rows(channels, n_c, n_y):
    frame = 2 * channels
    sample = np.arange(frame)
    window = 0.5 - 0.5 * np.cos(2 * np.pi / frame * sample)
    by_y = np.arange(n_c)[None, :] * n_y + np.arange(n_y)[:, None]
    by_z = by_y.reshape(n_y, -1, SIZE_X).transpose(1, 0, 2)
    scale = 1.0 / math.sqrt(3.0 * frame / 8.0)
    tables = []
    for channel in (by_y.reshape(-1), by_z.reshape(-1)):
        angle = 2 * np.pi / frame * (channel[:, None] * sample[None, :] % frame)
        table = np.concatenate([np.cos(angle), -np.sin(angle)], axis=0)
        tables.append(table * window[None, :] * scale)
    return jnp.asarray(np.stack(tables).astype(np.float32)).astype(BF16)


def far_first(size):
    return sorted(range(size), key=lambda d: -min(d, size - d))


def dot(a, b, dims):
    return lax.dot_general(a, b, dims, preferred_element_type=F32)


def rotate(x, k):
    lane = lax.broadcasted_iota(jnp.int32, x.shape, x.ndim - 1)
    index = (lane & ~(TB - 1)) | ((lane + k) & (TB - 1))
    return jnp.take_along_axis(x, index, axis=x.ndim - 1, mode="promise_in_bounds")


def kernel(
    n_c,
    n_y,
    volt_hbm,
    filt_hbm,
    wiring_hbm,
    pos_hbm,
    dir_hbm,
    gains_hbm,
    delays_hbm,
    made_ref,
    volt_ref,
    filt_ref,
    wiring_ref,
    pos_ref,
    dir_ref,
    gains_ref,
    delays_ref,
    a_spec,
    a_got,
    a_turn,
    a_col,
    b_spec,
    b_got,
    b_turn,
    b_col,
    tab_ref,
    dirs_ref,
    wre_ref,
    wim_ref,
    give_ref,
    take_ref,
    piece_ref,
    pow_ref,
    dm_ref,
    hot_ref,
    mean_ref,
    four_ref,
    gather_ref,
    shift_ref,
    in_sem,
    a_send,
    a_recv,
    b_send,
    b_recv,
    x_send,
    x_recv,
    p_send,
    p_recv,
    f_send,
    own_sem,
):
    c = lax.axis_index("crate")
    board = lax.axis_index("board")
    y = board // 2
    k = board % 2
    channels = n_c * n_y
    antennas = 8 * channels
    plane = 4 * channels
    beams = 16 * n_c
    half_beams = beams // 2
    half_c = n_c // 2
    partner = (c, 2 * y + 1 - k)
    n_x = SIZE_X
    n_z = n_c // n_x
    x = c % n_x
    z = c // n_x
    mine_at = y * n_c + c

    steps_c = [(dz, dx) for dz in range(n_z) for dx in range(n_x)]
    steps_c.sort(key=lambda s: -min(s[0], n_z - s[0]) - min(s[1], n_x - s[1]))
    crates = [(z + dz) % n_z * n_x + (x + dx) % n_x for dz, dx in steps_c[:-1]]
    places = [(y + dy) % n_y for dy in far_first(n_y)[:-1]]
    places_z = [(z + dz) % n_z for dz in far_first(n_z)[:-1]]
    places_x = [(x + dx) % n_x for dx in far_first(n_x)[:-1]]
    steps_yx = [(dy, dx) for dy in range(n_y) for dx in range(n_x)]
    steps_yx.sort(key=lambda s: -min(s[0], n_y - s[0]) - min(s[1], n_x - s[1]))
    places_yx = [(y + dy) % n_y * n_x + (x + dx) % n_x for dy, dx in steps_yx[:-1]]

    offset = pl.multiple_of(board // 4 * LANES, LANES)
    pairs = [
        (volt_hbm, volt_ref),
        (filt_hbm, filt_ref),
        (wiring_hbm, wiring_ref),
        (pos_hbm, pos_ref),
        (dir_hbm, dir_ref),
        (gains_hbm, gains_ref),
        (delays_hbm.at[:, pl.ds(offset, LANES)], delays_ref),
    ]
    loads = [pltpu.make_async_copy(*pair, in_sem.at[i]) for i, pair in enumerate(pairs)]
    for load in loads:
        load.start()

    barrier = pltpu.get_barrier_semaphore()
    near_ones = [(c, 2 * i + k) for i in places] + [(z * n_x + i, board) for i in places_x]
    near_ones += [(i * n_x + x, board) for i in places_z] + [partner]
    for device in near_ones:
        pl.semaphore_signal(barrier, inc=1, device_id=device, device_id_type=MESH)

    loads[0].wait()
    loads[1].wait()
    turned = jnp.swapaxes(volt_ref[...], 0, 1)
    frame_rows = turned.shape[0] // LOCAL_ANTENNAS

    def spectra(antenna):
        samples = jnp.concatenate(
            [turned[LOCAL_ANTENNAS * q + antenna] for q in range(frame_rows)], axis=1
        )
        rows = dot(filt_ref[antenna // 2], samples, NT)
        first, spec_ref = ((n_y, a_spec), (n_z, b_spec))[antenna // 2]
        rows = rows.reshape(2, first, channels // first, SPECTRA).astype(BF16)
        for part in range(2):
            spec_ref[antenna % 2, :, :, part * SPECTRA : (part + 1) * SPECTRA] = rows[part]

    spectra(0)
    spectra(2)

    def copy(src, dst, send, recv, device):
        return pltpu.make_async_remote_copy(
            src_ref=src,
            dst_ref=dst,
            send_sem=send,
            recv_sem=recv,
            device_id=device,
            device_id_type=MESH,
        )

    class Exchange:
        def __init__(self, src, dst, send, recv, own_sem, along):
            self.refs = (src, dst)
            self.sems = (send, recv)
            self.here, self.others, self.device = along
            own = (src.at[self.here], dst.at[self.here], own_sem)
            self.own = pltpu.make_async_copy(*own)
            count = pl.ds(0, len(self.others))
            self.all = copy(src.at[count], dst.at[count], send, recv, partner)

        def start(self):
            src, dst = self.refs
            for i in self.others:
                copy(src.at[i], dst.at[self.here], *self.sems, self.device(i)).start()
            self.own.start()

        def arrive(self):
            self.own.wait()
            self.all.wait_recv()

    along_y = (y, places, lambda i: (c, 2 * i + k))
    over_c = (c, crates, lambda i: (i, board))
    along_z = (z, places_z, lambda i: (i * n_x + x, board))
    over_yx = (y * n_x + x, places_yx, lambda i: (z * n_x + i % n_x, i // n_x * 2 + k))
    a_one, a_two, b_one, b_two = [], [], [], []
    for h in range(2):
        a_sems = [(a_send.at[s], a_recv.at[s], own_sem.at[s]) for s in (h, 2 + h)]
        b_sems = [(b_send.at[s], b_recv.at[s], own_sem.at[4 + s]) for s in (h, 2 + h)]
        a_one.append(Exchange(a_spec.at[h], a_got.at[h], *a_sems[0], along_y))
        a_two.append(Exchange(a_turn.at[h], a_col.at[h], *a_sems[1], over_c))
        b_one.append(Exchange(b_spec.at[h], b_got.at[h], *b_sems[0], along_z))
        b_two.append(Exchange(b_turn.at[h], b_col.at[h], *b_sems[1], over_yx))

    pl.semaphore_wait(barrier, len(near_ones))
    a_one[0].start()
    b_one[0].start()
    spectra(1)
    spectra(3)
    a_one[1].start()
    b_one[1].start()

    for load in loads[2:]:
        load.wait()
    shape = (plane // LANES, LANES)
    place = lax.broadcasted_iota(jnp.int32, shape, 0) * LANES
    place = place + lax.broadcasted_iota(jnp.int32, shape, 1)
    antenna = place // channels
    device = place % channels
    of_a = device // n_y * 2 * n_y + device % n_y * 2 + k
    crate = device % n_z * n_x + device % n_c // n_z
    of_b = crate * 2 * n_y + device // n_c * 2 + k
    row_id = jnp.where(antenna < 2, of_a, of_b) * 4 + antenna

    def look_up(index, row_of, dtype):
        group = index // LANES
        within = index % LANES
        found = jnp.zeros(shape, dtype)
        for h in range(antennas // LANES):
            row = jnp.broadcast_to(row_of(h), shape)
            got = jnp.take_along_axis(row, within, axis=1, mode="promise_in_bounds")
            found = jnp.where(group == h, got, found)
        return found

    def part_of(h):
        return slice(h * LANES, (h + 1) * LANES)

    ids = look_up(row_id, lambda h: wiring_ref[h : h + 1, :], jnp.int32)
    channel = c * n_y + y
    per_turn = 1.0 + channel.astype(F32) / channels
    norm = 1.0 / math.sqrt(antennas)
    own_row = lax.broadcasted_iota(jnp.int32, (n_y, LANES), 0) == y

    def gain_row(part, h):
        rows = gains_ref[part, :, part_of(h)]
        return jnp.sum(jnp.where(own_row, rows, 0.0), axis=0, keepdims=True)

    tab_ref[0] = look_up(ids, lambda h: pos_ref[0:1, part_of(h)], F32) * per_turn
    tab_ref[1] = look_up(ids, lambda h: pos_ref[1:2, part_of(h)], F32) * per_turn
    g_re = look_up(ids, lambda h: gain_row(0, h), F32) * norm
    g_im = look_up(ids, lambda h: gain_row(1, h), F32) * norm
    tab_ref[2] = g_re
    tab_ref[3] = g_im
    tab_ref[4] = 2.0 * g_re
    tab_ref[5] = 2.0 * g_im
    for i in range(2):
        dirs_ref[i] = jnp.broadcast_to(dir_ref[i : i + 1, :], (LANES, beams)).T

    sine, cosine = half_angle_coefficients()
    blocks = beams // ROWS

    def weights_block(i, carry):
        r = i // blocks
        first = pl.multiple_of(lax.rem(i, blocks) * ROWS, ROWS)
        columns = pl.ds(pl.multiple_of(r * LANES, LANES), LANES)
        px, py, gr, gi, gr2, gi2 = [tab_ref[n, pl.ds(r, 1), :] for n in range(6)]
        turns = dirs_ref[0, pl.ds(first, ROWS), :] * px + dirs_ref[1, pl.ds(first, ROWS), :] * py
        turn = turns - jnp.round(turns)
        square = turn * turn
        s = sine[-1]
        for coefficient in sine[-2::-1]:
            s = s * square + coefficient
        s = s * turn
        q = cosine[-1]
        for coefficient in cosine[-2::-1]:
            q = q * square + coefficient
        wre_ref[pl.ds(first, ROWS), columns] = (gr + s * (gi2 * q - gr2 * s)).astype(BF16)
        wim_ref[pl.ds(first, ROWS), columns] = (gi - s * (gi2 * s + gr2 * q)).astype(BF16)
        return carry

    steps = plane // LANES * blocks
    lax.fori_loop(0, steps // 2, weights_block, 0)
    for h in range(2):
        a_one[h].arrive()
        a_turn[h] = jnp.swapaxes(a_got[h], 0, 1)
        b_one[h].arrive()
        a_two[h].start()
        b_turn[h] = jnp.swapaxes(b_got[h], 0, 1)
        b_two[h].start()
    lax.fori_loop(steps // 2, steps, weights_block, 0)

    values = delays_ref[...].astype(F32).astype(BF16)
    source = lax.broadcasted_iota(jnp.int32, (channels, channels), 0)
    position = lax.broadcasted_iota(jnp.int32, (channels, channels), 1)
    tiles = channels // 4
    piece = position % tiles * 4 + position // tiles
    moved = (source == piece % n_c * n_y + piece // n_c).astype(F32).astype(BF16)
    dm_ref[...] = dot(values, moved, TN)
    mine = dm_ref[pl.ds(pl.multiple_of(board % 4 * TB, TB), TB), :]
    for d in range(TB):
        rows = slice(d % 8 * TB, (d % 8 + 1) * TB)
        hot_ref[rows, d // 8 * channels : (d // 8 + 1) * channels] = (
            (mine == float(d)).astype(F32).astype(BF16)
        )

    chunks = 2
    size = half_beams // chunks
    served = half_c // chunks

    from_s = lax.broadcasted_iota(jnp.int32, (SPECTRA, LANES), 0)
    to_t = lax.broadcasted_iota(jnp.int32, (SPECTRA, LANES), 1)
    mean = jnp.where(from_s // AVG == to_t % TB, 1.0 / AVG, 0.0).astype(BF16)
    beam = lax.broadcasted_iota(jnp.int32, (size, LANES), 0)
    slot = lax.broadcasted_iota(jnp.int32, (size, LANES), 1)
    to_row = lax.broadcasted_iota(jnp.int32, (size // 4, size), 0)
    of_beam = lax.broadcasted_iota(jnp.int32, (size // 4, size), 1)
    gather = (of_beam // 4 == to_row).astype(F32).astype(BF16)
    mean_ref[...] = mean
    four_ref[...] = jnp.where(beam % 4 == slot // TB, 1.0, 0.0)
    gather_ref[...] = gather
    for n in range(3):
        chosen = from_s == to_t // TB * TB + (to_t + 8 * n + 8) % TB
        shift_ref[:, n * LANES : (n + 1) * LANES] = chosen.astype(F32).astype(BF16)

    for h in range(2):
        a_two[h].arrive()
        b_two[h].arrive()

    rows = (2 * channels, 2 * SPECTRA)
    columns = jnp.concatenate([a_col[...].reshape(rows), b_col[...].reshape(rows)], axis=0)

    def beams_of(which, h):
        rows = pl.ds(pl.multiple_of(which * half_beams + h * size, size), size)
        with_re = dot(wre_ref[rows, :], columns, NN)
        with_im = dot(wim_ref[rows, :], columns, NN)
        return (
            with_re[:, :SPECTRA] - with_im[:, SPECTRA:],
            with_re[:, SPECTRA:] + with_im[:, :SPECTRA],
        )

    swaps = []
    for h in range(chunks):
        give_ref[h, 0], give_ref[h, 1] = beams_of(1 - k, h)
        swaps.append(copy(give_ref.at[h], take_ref.at[h], x_send.at[h], x_recv.at[h], partner))
        swaps[h].start()

    kept = [beams_of(k, h) for h in range(chunks)]

    def powers(h):
        keep_re, keep_im = kept[h]
        swaps[h].wait_recv()
        beam_re = keep_re + take_ref[h, 0]
        beam_im = keep_im + take_ref[h, 1]
        energy = beam_re * beam_re + beam_im * beam_im
        high = energy.astype(BF16)
        low = (energy - high.astype(F32)).astype(BF16)
        power = dot(high, mean_ref[...], NN) + dot(low, mean_ref[...], NN)
        power = jnp.where(four_ref[...] > 0.0, power, 0.0).astype(BF16)
        rows = dot(gather_ref[...], power, NN).reshape(served, 4, LANES)
        piece_ref[h * served : (h + 1) * served] = rows.astype(BF16)

    holds = c // half_c == k
    count = half_c * n_y

    def p_copy(index, to_y):
        return copy(
            piece_ref.at[index],
            pow_ref.at[mine_at],
            p_send,
            p_recv.at[y],
            (k * half_c + index, 2 * to_y + k),
        )

    for h in range(chunks):
        powers(h)
        tails = [h * served + (x + dx) % n_x for dx in far_first(n_x)]
        indices = [i + tail for tail in tails for i in range(0, served, n_x)]
        for to_y in places:
            for index in indices:
                p_copy(index, to_y).start()
        for index in indices:

            @pl.when(k * half_c + index != c)
            def _():
                p_copy(index, y).start()

    def group(source, size):
        return pow_ref.at[pl.ds(pl.multiple_of(source * n_c, n_c), size)]

    def forward(source):
        rows = group(source, n_c)
        return copy(rows, rows, f_send.at[source], p_recv.at[source], partner)

    def group_wait(source, size):
        rows = group(source, size)
        copy(rows, rows, p_send, p_recv.at[source], partner).wait_recv()

    @pl.when(holds)
    def _():
        own_p = pltpu.make_async_copy(
            piece_ref.at[lax.rem(c, half_c)], pow_ref.at[mine_at], own_sem.at[8]
        )
        own_p.start()
        own_p.wait()
        group_wait(y, n_c - 1)
        forward(y).start()

        def g_wait(i, carry):
            source = lax.rem(y + i, n_y)
            group_wait(source, n_c)
            forward(source).start()
            return carry

        lax.fori_loop(1, n_y, g_wait, 0)

    @pl.when(jnp.logical_not(holds))
    def _():
        def f_wait(i, carry):
            forward(i).wait_recv()
            return carry

        lax.fori_loop(0, n_y, f_wait, 0)

    series = jnp.swapaxes(pow_ref[...].reshape(tiles, 16, LANES), 0, 1)
    flat = series.reshape(16 * tiles, LANES)
    near = dot(flat, shift_ref[:, : 2 * LANES], NN).astype(BF16)
    shifted = [flat, near[:, :LANES], near[:, LANES:], dot(flat, shift_ref[:, 2 * LANES :], NN).astype(BF16)]
    shifted = [v.reshape(16, tiles, LANES) for v in shifted]
    for pair in range(2):
        both = [
            jnp.concatenate([v[4 * r + 2 * pair + j] for v in shifted for r in range(4)], axis=0)
            for j in range(2)
        ]
        sums = dot(hot_ref[...], jnp.concatenate(both, axis=1), NN)
        mean_of = []
        for j in range(2):
            level = dot(jnp.ones((8, channels), BF16), both[j][:channels], NN)
            step = TB // 2
            while step:
                level = level + rotate(level, step)
                step //= 2
            mean_of.append(level[:1] * (1.0 / TB))
        for j in range(2):
            total = sums[:, j * LANES : (j + 1) * LANES]
            step = 4
            while step:
                rows = step * TB
                total = total[:rows] + rotate(total[rows:], step)
                step //= 2
            result = (total - mean_of[j]) * (1.0 / math.sqrt(channels))
            first = 4 * (2 * pair + j)
            for q in range(4):
                made_ref[first + q] = result[:, q * TB : (q + 1) * TB]

    for one in a_one + a_two + b_one + b_two:
        one.all.wait_send()
    for swap in swaps:
        swap.wait_send()

    @pl.when(holds)
    def _():
        rows = pow_ref.at[pl.ds(0, count - 1)]
        copy(rows, rows, p_send, p_recv.at[0], partner).wait_send()

        def f_sent(i, carry):
            forward(i).wait_send()
            return carry

        lax.fori_loop(0, n_y, f_sent, 0)

    @pl.when(jnp.logical_not(holds))
    def _():
        rows = pow_ref.at[pl.ds(0, count)]
        copy(rows, rows, p_send, p_recv.at[0], partner).wait_send()


def shards(n_c, n_y, voltages, wiring, positions, directions, gains, delays):
    channels = n_c * n_y
    frame = 2 * channels
    plane = 4 * channels
    beams = 16 * n_c
    half_beams = beams // 2
    samples = voltages.reshape(LOCAL_ANTENNAS, SPECTRA * frame // LANES, LANES).transpose(1, 0, 2)
    samples = samples.reshape(SPECTRA, frame // LANES * LOCAL_ANTENNAS, LANES)
    table = filter_rows(channels, n_c, n_y)
    ids = wiring.reshape(-1, LANES)
    operands = (samples, table, ids, positions, directions, gains, delays)
    loaded = [pltpu.VMEM(x.shape, x.dtype) for x in operands[:-1]]
    loaded.append(pltpu.VMEM((channels, LANES), delays.dtype))
    dma = pltpu.SemaphoreType.DMA
    by_y = pltpu.VMEM((2, n_y, n_c, 2 * SPECTRA), BF16)
    by_c = pltpu.VMEM((2, n_c, n_y, 2 * SPECTRA), BF16)
    n_z = n_c // SIZE_X
    chunks = 2
    by_z = pltpu.VMEM((2, n_z, channels // n_z, 2 * SPECTRA), BF16)
    by_yx = pltpu.VMEM((2, channels // n_z, n_z, 2 * SPECTRA), BF16)
    return pl.pallas_call(
        functools.partial(kernel, n_c, n_y),
        out_shape=pltpu.VMEM((16, TB, TB), F32),
        in_specs=[pl.BlockSpec(memory_space=pl.ANY)] * len(operands),
        out_specs=pl.BlockSpec(memory_space=pltpu.VMEM),
        scratch_shapes=[
            *loaded,
            *[by_y, by_y, by_c, by_c],
            *[by_z, by_z, by_yx, by_yx],
            pltpu.VMEM((6, plane // LANES, LANES), F32),
            pltpu.VMEM((2, beams, LANES), F32),
            pltpu.VMEM((beams, plane), BF16),
            pltpu.VMEM((beams, plane), BF16),
            *[pltpu.VMEM((chunks, 2, half_beams // chunks, SPECTRA), F32)] * 2,
            pltpu.VMEM((n_c // 2, 4, LANES), BF16),
            pltpu.VMEM((channels, 4, LANES), BF16),
            pltpu.VMEM((LANES, channels), F32),
            pltpu.VMEM((8 * TB, 4 * channels), BF16),
            pltpu.VMEM((SPECTRA, LANES), BF16),
            pltpu.VMEM((half_beams // chunks, LANES), F32),
            pltpu.VMEM((half_beams // chunks // 4, half_beams // chunks), BF16),
            pltpu.VMEM((LANES, 3 * LANES), BF16),
            dma((len(operands),)),
            *[dma((4,))] * 4,
            *[dma((chunks,))] * 2,
            dma,
            dma((n_y,)),
            dma((n_y,)),
            dma((9,)),
        ],
        compiler_params=pltpu.CompilerParams(
            collective_id=0, has_side_effects=True, vmem_limit_bytes=60 * 1024 * 1024
        ),
    )(*operands)


def solution(mesh):
    n_c = mesh.shape["crate"]
    n_y = mesh.shape["board"] // 2
    in_specs = (P(("crate", "board"), None), P(), P(), P(), P(None, "crate", None), P())
    return jax.shard_map(
        functools.partial(shards, n_c, n_y),
        mesh=mesh,
        in_specs=in_specs,
        out_specs=P("crate", "board", None),
        check_vma=False,
    )
```
